32 devices in a mesh: parts: 2 (over y), tiles: 8 (over z, x), mesh: 2 (over core).
Axes of the slice: x: 2, y: 2, z: 4, core: 2. Of those that a mesh axis runs over, the one named last changes fastest.
Arguments:
- patches: bfloat16 [1024, 128, 128], P(('parts', 'tiles', 'mesh')), parts along dimension 0, may hold values from -6 to 6
- send_index: int32 [32, 32], P(('parts', 'tiles', 'mesh')), parts along dimension 0, may hold values from 0 to 32, as said below
- pair_slots: int32 [32, 2, 16], P(('parts', 'tiles', 'mesh')), parts along dimension 0, may hold values from 0 to 32, as said below
- node_links: int32 [32, 4, 128], P(('parts', 'tiles', 'mesh')), parts along dimension 0, may hold values from 0 to 31
Outputs:
- pair_flow: float32 [2, 512], P(None, ('parts', 'tiles', 'mesh')), parts along dimension 1
- relaxed: float32 [2, 4096], P(None, ('parts', 'tiles', 'mesh')), parts along dimension 1
The draws below stay inside these ranges and needn't reach their ends.
There are 2 independent parts, one for each index of `parts`. The reference program is written for one: setup_inputs(seed, part) draws one part's arguments, and reference() takes and returns one part's arrays. A program takes and returns all parts, laid end to end along the dimension named above; each array names one. Nothing has to cross between parts.
Inputs may be any that keep to these rules, and one draw needn't show every extreme that they name: `send_index`: each patch is sent to at most one owner, as one side of one tile pair; a live pair's two sides come from two different tiles and pair_slots names their received slots, numbered source tile times 4 plus slot; the value 2 * 16 marks an empty send slot. Some device fills all 4 slots to one peer. `pair_slots`: the value 8 * 4 marks a pair slot without a live pair; the number of live pairs differs from owner to owner, and some owner has all 16 slots live.
All inputs are finite; a program needn't handle non-finite values.
Results may differ from the reference program's by a relative error of at most 0.011.
Values may be sent and summed in bfloat16 or wider, within the bound.
No kernel may reach another device: no remote copies, remote signals or barrier semaphores. Data moves between devices by JAX's collectives and lax.ppermute only.
A program may use at most 64 MiB of HBM per device.

```python
import math
import jax
import jax.numpy as jnp
from jax import lax

PATCH = 128
PAIR_DEV = 16
NODE_DEV = 128
LINKS = 4
PATCHES_DEV = 32
DEVS = 16
N_TILES = 8
N_MESH = 2


def routing_tables(key):
    tile_count = N_TILES
    mesh_count = N_MESH
    pair_count = PAIR_DEV
    capacity = (2 * pair_count + tile_count - 1) // tile_count
    empty_patch = 2 * pair_count
    empty_slot = tile_count * capacity
    sides = jnp.arange(2 * pair_count, dtype=jnp.int32)
    owners = jnp.arange(tile_count, dtype=jnp.int32)
    base_key = jax.random.fold_in(key, 7)

    def one_column(column_key):
        keys = jax.random.split(column_key, 3)
        order = jax.random.permutation(keys[0], tile_count).astype(jnp.int32)
        offset = jax.random.permutation(keys[1], tile_count).astype(jnp.int32)
        counts = jax.random.randint(keys[2], (tile_count,), 3 * pair_count // 4, pair_count + 1).astype(jnp.int32)
        counts = counts.at[0].set(pair_count)
        places = (offset[:, None] + sides[None, :]) % tile_count
        sender = order[places]
        round_of = sides // tile_count
        pair_of = sides // 2
        live = pair_of[None, :] < counts[:, None]
        send_col = owners[:, None] * capacity + round_of[None, :]
        sends = jnp.full((tile_count, tile_count * capacity), empty_patch, jnp.int32)
        sends = sends.at[sender, send_col].set(jnp.where(live, sides[None, :], empty_patch))
        slot_value = jnp.where(live, sender * capacity + round_of[None, :], empty_slot)
        paired = slot_value.reshape(tile_count, pair_count, 2)
        slots = jnp.stack([paired[:, :, 1], paired[:, :, 0]], axis=1)
        return (sends, slots)
    column_keys = jax.vmap(lambda number: jax.random.fold_in(base_key, number))(jnp.arange(mesh_count, dtype=jnp.int32))
    sends, slots = jax.vmap(one_column)(column_keys)
    sends = jnp.swapaxes(sends, 0, 1).reshape(tile_count * mesh_count, tile_count * capacity)
    slots = jnp.swapaxes(slots, 0, 1).reshape(tile_count * mesh_count, 2, pair_count)
    return (sends.astype(jnp.int32), slots.astype(jnp.int32))


def draw_send_index(key, part):
    return routing_tables(key)[0]


def draw_pair_slots(key, part):
    return routing_tables(key)[1]


def touch_ends(array, key, least, largest):
    longest = array.shape.index(max(array.shape))
    spots = []
    for shift in (0, 1):
        where = [jax.random.randint(jax.random.fold_in(key, axis), (), 0, length) for axis, length in enumerate(array.shape)]
        where[longest] = (where[longest] + shift) % array.shape[longest]
        spots.append(tuple(where))
    return array.at[spots[0]].set(least).at[spots[1]].set(largest)


def level_of(own_key, dims, pieces, smallest, high):
    loudness = 1.0
    for position, blocks in pieces:
        draws = jax.random.uniform(jax.random.fold_in(jax.random.fold_in(own_key, 6), position), (blocks,), jnp.float32, smallest / len(pieces), high / len(pieces))
        loudness = loudness * jnp.repeat(jnp.exp(draws), dims[position] // blocks).reshape((-1,) + (1,) * (len(dims) - 1 - position))
    return loudness


def noise(stream_key, extent, spread, reach, cuts=(), held_as=jnp.bfloat16):
    loudness = level_of(stream_key, extent, cuts, -0.22, 0.18) if cuts else 1.0
    array = jax.random.normal(stream_key, extent, jnp.float32) * spread * loudness
    return jnp.minimum(jnp.maximum(array, -reach), reach).astype(held_as)


def setup_inputs(seed: int = 0, part: int = 0) -> dict:
    streams_of = jax.random.split(jax.random.key(seed), 5)
    part_keys = jax.random.split(jax.random.fold_in(streams_of[4], part), 5)
    return {
        "patches": noise(part_keys[0], (DEVS * PATCHES_DEV, PATCH, PATCH), 1.0, 6.0, ((0, 16),)),
        "send_index": draw_send_index(jax.random.fold_in(jax.random.fold_in(streams_of[4], part), 71), part),
        "pair_slots": draw_pair_slots(jax.random.fold_in(jax.random.fold_in(streams_of[4], part), 71), part),
        "node_links": touch_ends(jax.random.randint(part_keys[3], (DEVS, LINKS, NODE_DEV), 0, N_MESH * PAIR_DEV), jax.random.fold_in(part_keys[3], 1), 0, (N_MESH * PAIR_DEV) - 1).astype(jnp.int32),
    }


def make_tables(side_len):
    ticks = jnp.arange(side_len, dtype=jnp.int32)
    product = ticks[:, None] * ticks[None, :] % side_len
    angle = 2.0 * math.pi / side_len * product.astype(jnp.float32)
    cosine = jnp.cos(angle) / math.sqrt(side_len)
    sine = jnp.sin(angle) / math.sqrt(side_len)
    coord = ticks.astype(jnp.float32)
    gap = coord[:, None] - coord[None, :]
    narrow = jnp.exp(-gap * gap / (2.0 * 0.35 * 0.35)) / (0.35 * math.sqrt(2.0 * math.pi))
    broad = jnp.exp(-gap * gap / 32.0) / (4.0 * math.sqrt(2.0 * math.pi))
    band = narrow - broad
    lag = jnp.where(coord < side_len / 2, coord, coord - side_len)
    return (cosine.astype(jnp.bfloat16), sine.astype(jnp.bfloat16), band.astype(jnp.bfloat16), lag)

def high_dot(form, left, right):
    return jnp.einsum(form, left.astype(jnp.float32), right.astype(jnp.float32), precision=lax.Precision.HIGHEST)

def band_pass(stack, band):
    partial_value = high_dot('ij,bjk->bik', band, stack).astype(jnp.bfloat16)
    return high_dot('bij,kj->bik', partial_value, band).astype(jnp.bfloat16)

def spectral_flow(filtered, tables):
    cosine, sine, band, lag = tables
    side_len = filtered.shape[-1]
    count = filtered.shape[0] // 2
    left = jnp.concatenate([cosine, sine], 0)
    right = jnp.concatenate([cosine, sine], 1)
    back_left = jnp.concatenate([cosine, -sine], 1)
    halves = high_dot('ij,bjk->bik', left, filtered).astype(jnp.bfloat16)
    quarter = high_dot('bij,jk->bik', halves, right)
    real_part = quarter[:, :side_len, :side_len] - quarter[:, side_len:, side_len:]
    imag_part = -(quarter[:, :side_len, side_len:] + quarter[:, side_len:, :side_len])
    moving_real, fixed_real = (real_part[:count], real_part[count:])
    moving_imag, fixed_imag = (imag_part[:count], imag_part[count:])
    power_real = moving_real * fixed_real + moving_imag * fixed_imag
    power_imag = moving_imag * fixed_real - moving_real * fixed_imag
    power = jnp.concatenate([power_real, power_imag], 1).astype(jnp.bfloat16)
    mixed = high_dot('bij,jk->bik', power, right)
    first = mixed[:, :side_len, :side_len] - mixed[:, side_len:, side_len:]
    second = mixed[:, :side_len, side_len:] + mixed[:, side_len:, :side_len]
    stacked = jnp.concatenate([first, second], 1).astype(jnp.bfloat16)
    surface = high_dot('ij,bjk->bik', back_left, stacked)
    weight = surface * surface
    denom = lax.optimization_barrier(jnp.mean(weight, axis=(1, 2))) + 1e-06
    flow_y = lax.optimization_barrier(jnp.mean(lag[None, :, None] * weight, axis=(1, 2))) / denom
    flow_x = lax.optimization_barrier(jnp.mean(lag[None, None, :] * weight, axis=(1, 2))) / denom
    return jnp.stack([flow_y, flow_x], 0)

def reference(patches, send_index, pair_slots, node_links):
    tables = make_tables(PATCH)
    tile_count = N_TILES
    mesh_count = N_MESH
    pair_count = PAIR_DEV
    patch_count = 2 * pair_count
    capacity = send_index.shape[1] // tile_count
    empty_slot = tile_count * capacity
    devices = tile_count * mesh_count

    def owner_flows(owner):
        tile = owner // mesh_count
        lane = owner % mesh_count
        slots = pair_slots[owner]
        valid = slots < empty_slot
        safe = jnp.minimum(slots, empty_slot - 1)
        source = (safe // capacity * mesh_count + lane).astype(jnp.int32)
        local = send_index[source, tile * capacity + safe % capacity]
        valid = valid & (local < patch_count)
        flat = (source * patch_count + jnp.minimum(local, patch_count - 1)).astype(jnp.int32)
        chosen = patches[flat.reshape(-1)]
        chosen = jnp.where(valid.reshape(-1)[:, None, None], chosen, jnp.zeros_like(chosen))
        filtered = band_pass(chosen, tables[2])
        return spectral_flow(filtered, tables)
    all_flows = lax.map(owner_flows, jnp.arange(devices, dtype=jnp.int32))
    pair_flow = jnp.transpose(all_flows, (1, 0, 2)).reshape(2, devices * pair_count)
    group = all_flows.reshape(tile_count, mesh_count, 2, pair_count)
    group = jnp.transpose(group, (0, 2, 1, 3)).reshape(tile_count, 2, mesh_count * pair_count)
    tile_of = jnp.arange(devices, dtype=jnp.int32) // mesh_count

    def relax_one(flow_rows, links):
        linked = flow_rows[:, links]
        return 0.5 * linked[:, 0] + 0.5 * lax.optimization_barrier(jnp.mean(linked[:, 1:], axis=1))
    relaxed = jax.vmap(relax_one)(group[tile_of], node_links)
    relaxed = jnp.transpose(relaxed, (1, 0, 2)).reshape(2, devices * NODE_DEV)
    return (pair_flow, relaxed)
```

```python
import functools
import math

import jax
import jax.numpy as jnp
import numpy as np
from jax import lax
from jax.experimental import pallas as pl
from jax.experimental.pallas import tpu as pltpu
from jax.sharding import PartitionSpec as P


F32 = jnp.float32
BF16 = jnp.bfloat16
ANY = pl.BlockSpec(memory_space=pl.ANY)
SMEM = pl.BlockSpec(memory_space=pltpu.SMEM)
VMEM = pl.BlockSpec(memory_space=pltpu.VMEM)
DIRECT_LIMIT = 16


def make_tables(side):
    ticks = np.arange(side)
    angle = 2.0 * np.pi / side * (ticks[:, None] * ticks[None, :] % side)
    cosine = np.cos(angle) / math.sqrt(side)
    sine = np.sin(angle) / math.sqrt(side)
    gap = (ticks[:, None] - ticks[None, :]).astype(np.float64)
    narrow = np.exp(-gap * gap / (2.0 * 0.35 * 0.35)) / (0.35 * math.sqrt(2.0 * math.pi))
    broad = np.exp(-gap * gap / 32.0) / (4.0 * math.sqrt(2.0 * math.pi))
    band = narrow - broad

    def const(array):
        return jnp.asarray(array.astype(np.float32)).astype(BF16)

    left = const(np.concatenate([cosine, sine], 0))
    right = const(np.concatenate([cosine, sine], 1))
    back = const(np.concatenate([cosine, -sine], 1))
    return const(band), left, right, back


def dot(a, b):
    return jnp.dot(a, b, preferred_element_type=F32)


def offsets(count):
    half = count // 2
    order = [half]
    for step in range(1, half):
        order += [half - step, half + step]
    if count > 1 and count % 2:
        order.append(count - 1)
    order = [d for d in dict.fromkeys(order) if 0 < d < count]
    return order + [d for d in range(1, count) if d not in order]


def pick_kernel(order, cap, send_ref, patches_ref, *rest):
    outs, (zero, sems) = rest[:-2], rest[-2:]
    count = len(order)
    me = lax.axis_index("tiles")
    limit = patches_ref.shape[0]
    zero[...] = jnp.zeros_like(zero)
    for k, d in enumerate(order):
        peer = lax.rem(me + d, count)
        for s in range(cap):
            index = send_ref[0, peer * cap + s]
            there = outs[k].at[s]
            sem = sems.at[k * cap + s]

            @pl.when(index < limit)
            def _():
                pltpu.make_async_copy(patches_ref.at[index], there, sem).start()

            @pl.when(index >= limit)
            def _():
                pltpu.make_async_copy(zero, there, sem).start()

    for k in range(count):
        for s in range(cap):
            pltpu.make_async_copy(zero, outs[k].at[s], sems.at[k * cap + s]).wait()


def pick(patches, send_index, order, cap):
    side = patches.shape[-1]
    out = [jax.ShapeDtypeStruct((cap, side, side), patches.dtype)] * len(order)
    return pl.pallas_call(
        functools.partial(pick_kernel, order, cap),
        out_shape=out,
        in_specs=[SMEM, ANY],
        out_specs=[ANY] * len(order),
        scratch_shapes=[
            pltpu.VMEM((side, side), patches.dtype),
            pltpu.SemaphoreType.DMA((len(order) * cap,)),
        ],
        name="pick",
    )(send_index, patches)


def spectra(x, band, left, right):
    cap, side = x.shape[0], x.shape[-1]
    partial = jnp.concatenate([dot(band, x[s]).astype(BF16) for s in range(cap)], 0)
    filtered = lax.dot_general(
        partial, band, (((1,), (1,)), ((), ())), preferred_element_type=F32
    ).astype(BF16)
    result = []
    for s in range(cap):
        halves = dot(left, filtered[s * side : (s + 1) * side]).astype(BF16)
        quarter = dot(halves, right)
        real = quarter[:side, :side] - quarter[side:, side:]
        imag = -(quarter[:side, side:] + quarter[side:, :side])
        result.append((real, imag))
    return result


def sums(mr, mi, fr, fi, sign, right, back):
    side = mr.shape[-1]
    power_real = mr * fr + mi * fi
    power_imag = mi * fr - mr * fi
    if sign is not None:
        power_imag = power_imag * sign
    power = jnp.concatenate([power_real, power_imag], 0).astype(BF16)
    mixed = dot(power, right)
    first = mixed[:side, :side] - mixed[side:, side:]
    second = mixed[:side, side:] + mixed[side:, :side]
    stacked = jnp.concatenate([first, second], 0).astype(BF16)
    surface = dot(back, stacked)
    weight = surface * surface
    row = lax.broadcasted_iota(jnp.int32, (side, side), 0).astype(F32)
    lag = jnp.where(row < side / 2, row, row - side)
    return jnp.sum(weight, 0, keepdims=True), jnp.sum(lag * weight, 0, keepdims=True)


def flows_of(parts, side):
    plain = jnp.concatenate([p[0] for p in parts], 0)
    by_row = jnp.concatenate([p[1] for p in parts], 0)
    column = lax.broadcasted_iota(jnp.int32, plain.shape, 1).astype(F32)
    lag = jnp.where(column < side / 2, column, column - side)
    scale = 1.0 / (side * side)
    denom = jnp.sum(plain, 1, keepdims=True) * scale + 1e-06
    flow_y = jnp.sum(by_row, 1, keepdims=True) * scale / denom
    flow_x = jnp.sum(plain * lag, 1, keepdims=True) * scale / denom
    return flow_y, flow_x


def main_kernel(order, cap, group, slots_ref, links_ref, band, left, right, back, *rest):
    count = len(order)
    early = count - 1
    chunks = rest[:early]
    flow_ref, other_ref, meta_ref, mix_ref, held, spec, sems = rest[early:]
    side = held.shape[-1]
    pairs = slots_ref.shape[-1]
    me = lax.axis_index("tiles")
    total = count * cap

    copies = [
        pltpu.make_async_copy(chunks[k], held.at[k], sems.at[k]) for k in range(early)
    ]
    for copy in copies:
        copy.start()

    row = lax.broadcasted_iota(jnp.int32, mix_ref.shape, 0)
    links = links_ref.shape[1]
    mix = jnp.zeros(mix_ref.shape, F32)
    for k in range(links):
        share = 0.5 if k == 0 else 0.5 / (links - 1)
        mix += jnp.where(row == links_ref[0, k : k + 1, :], share, 0.0)
    mix_ref[...] = mix

    last = lax.rem(me - order[-1] + count, count)
    rank = [0] * count
    for k, d in enumerate(order):
        rank[d] = k

    def place(slot):
        off = lax.rem(me - slot // cap + count, count)
        pos = jnp.int32(0)
        for d in range(count):
            pos = jnp.where(off == d, rank[d], pos)
        return jnp.where(slot < total, pos * cap + slot % cap, total)

    for s in range(cap):
        meta_ref[0, s] = -1
        meta_ref[1, s] = 0
        meta_ref[2, s] = total
    for q in range(pairs):
        a, b = slots_ref[0, 0, q], slots_ref[0, 1, q]

        @pl.when((a < total) & (a // cap == last))
        def _():
            meta_ref[0, a % cap] = q
            meta_ref[1, a % cap] = 1
            meta_ref[2, a % cap] = place(b)

        @pl.when((b < total) & (b // cap == last))
        def _():
            meta_ref[0, b % cap] = q
            meta_ref[1, b % cap] = -1
            meta_ref[2, b % cap] = place(a)

    spec[early * cap :] = jnp.zeros((spec.shape[0] - early * cap,) + spec.shape[1:], F32)

    for copy in copies:
        copy.wait()

    @pl.loop(0, early)
    def _(k):
        for s, (real, imag) in enumerate(spectra(held[k], band[...], left[...], right[...])):
            spec[k * cap + s, 0] = real
            spec[k * cap + s, 1] = imag

    @pl.loop(0, pairs // group)
    def _(g):
        parts = []
        for j in range(group):
            a = place(slots_ref[0, 0, g * group + j])
            b = place(slots_ref[0, 1, g * group + j])
            parts.append(
                sums(spec[a, 0], spec[a, 1], spec[b, 0], spec[b, 1], None, right[...], back[...])
            )
        flow_y, flow_x = flows_of(parts, side)
        for j in range(group):
            at = pl.ds(g * group + j, 1)
            flow_ref[0, at] = jnp.broadcast_to(flow_y[j : j + 1], (1, side))
            flow_ref[1, at] = jnp.broadcast_to(flow_x[j : j + 1], (1, side))

    for s in range(cap):
        other_ref[s] = spec[meta_ref[2, s]]


def last_kernel(x, flow_in, other, meta_ref, band, left, right, back, flow_ref):
    cap, side = x.shape[0], x.shape[-1]
    pairs = flow_in.shape[1]
    parts = []
    for s, (real, imag) in enumerate(spectra(x[...], band[...], left[...], right[...])):
        sign = meta_ref[1, s].astype(F32)
        parts.append(sums(real, imag, other[s, 0], other[s, 1], sign, right[...], back[...]))
    flow_y, flow_x = flows_of(parts, side)
    row = lax.broadcasted_iota(jnp.int32, (pairs, side), 0)
    out_y, out_x = flow_in[0], flow_in[1]
    for s in range(cap):
        hit = row == meta_ref[0, s]
        out_y = jnp.where(hit, flow_y[s : s + 1], out_y)
        out_x = jnp.where(hit, flow_x[s : s + 1], out_x)
    flow_ref[0] = out_y
    flow_ref[1] = out_x


def relax_kernel(flow_ref, mix_ref, out_ref):
    mix = mix_ref[...]
    rows = []
    for c in range(2):
        flow = jnp.concatenate([flow_ref[m, c] for m in range(flow_ref.shape[0])], 0)
        rows.append(jnp.sum(flow * mix, 0, keepdims=True))
    out_ref[...] = jnp.concatenate(rows, 0)


def direct(patches, send_index, pair_slots, node_links):
    side = patches.shape[-1]
    pairs = pair_slots.shape[-1]
    nodes = node_links.shape[-1]
    count = lax.axis_size("tiles")
    meshes = lax.axis_size("mesh")
    cap = send_index.shape[-1] // count
    order = [0] + offsets(count)
    tables = make_tables(side)
    picked = pick(patches, send_index, order, cap)
    chunks = [picked[0]]
    for k in range(1, count):
        d = order[k]
        path = [(i, (i + d) % count) for i in range(count)]
        chunks.append(lax.ppermute(picked[k], "tiles", path))
    group = 4 if pairs % 4 == 0 else 1
    flow, other, meta, mix = pl.pallas_call(
        functools.partial(main_kernel, order, cap, group),
        out_shape=[
            jax.ShapeDtypeStruct((2, pairs, side), F32),
            jax.ShapeDtypeStruct((cap, 2, side, side), F32),
            jax.ShapeDtypeStruct((3, cap), jnp.int32),
            jax.ShapeDtypeStruct((meshes * pairs, nodes), F32),
        ],
        in_specs=[SMEM] + [VMEM] * 5 + [ANY] * (count - 1),
        out_specs=[VMEM, VMEM, SMEM, VMEM],
        scratch_shapes=[
            pltpu.VMEM((count - 1, cap, side, side), BF16),
            pltpu.VMEM((count * cap + 1, 2, side, side), F32),
            pltpu.SemaphoreType.DMA((count - 1,)),
        ],
        name="main",
    )(pair_slots, node_links, *tables, *chunks[:-1])
    flow = pl.pallas_call(
        last_kernel,
        out_shape=jax.ShapeDtypeStruct((2, pairs, side), F32),
        in_specs=[VMEM, VMEM, VMEM, SMEM] + [VMEM] * 4,
        out_specs=VMEM,
        name="last",
    )(chunks[-1], flow, other, meta, *tables)
    both = lax.all_gather(flow, "mesh")
    relaxed = pl.pallas_call(
        relax_kernel,
        out_shape=jax.ShapeDtypeStruct((2, nodes), F32),
        in_specs=[VMEM, VMEM],
        out_specs=VMEM,
        name="relax",
    )(both, mix)
    return flow[:, :, 0], relaxed


def general(patches, send_index, pair_slots, node_links):
    side = patches.shape[-1]
    held = patches.shape[0]
    pairs = pair_slots.shape[-1]
    count = lax.axis_size("tiles")
    band, left, right, back = make_tables(side)
    wanted = send_index[0]
    cap = wanted.shape[0] // count
    picked = patches[jnp.minimum(wanted, held - 1)]
    picked = jnp.where((wanted < held)[:, None, None], picked, jnp.zeros_like(picked))
    received = lax.all_to_all(
        picked.reshape((count, cap) + patches.shape[1:]), "tiles", 0, 0, tiled=True
    )
    total = count * cap
    received = received.reshape((total,) + received.shape[2:])
    slots = pair_slots[0].reshape(-1)
    chosen = received[jnp.minimum(slots, total - 1)]
    chosen = jnp.where((slots < total)[:, None, None], chosen, jnp.zeros_like(chosen))

    def mul(form, a, b):
        return jnp.einsum(form, a, b, preferred_element_type=F32)

    partial = mul("ij,bjk->bik", band, chosen).astype(BF16)
    filtered = mul("bij,kj->bik", partial, band).astype(BF16)
    halves = mul("ij,bjk->bik", left, filtered).astype(BF16)
    quarter = mul("bij,jk->bik", halves, right)
    real = quarter[:, :side, :side] - quarter[:, side:, side:]
    imag = -(quarter[:, :side, side:] + quarter[:, side:, :side])
    mr, fr, mi, fi = real[:pairs], real[pairs:], imag[:pairs], imag[pairs:]
    power = jnp.concatenate([mr * fr + mi * fi, mi * fr - mr * fi], 1).astype(BF16)
    mixed = mul("bij,jk->bik", power, right)
    first = mixed[:, :side, :side] - mixed[:, side:, side:]
    second = mixed[:, :side, side:] + mixed[:, side:, :side]
    stacked = jnp.concatenate([first, second], 1).astype(BF16)
    weight = mul("ij,bjk->bik", back, stacked) ** 2
    lag = jnp.asarray(np.where(np.arange(side) < side / 2, 0, -side) + np.arange(side), F32)
    denom = jnp.mean(weight, axis=(1, 2)) + 1e-06
    flow_y = jnp.mean(lag[None, :, None] * weight, axis=(1, 2)) / denom
    flow_x = jnp.mean(lag[None, None, :] * weight, axis=(1, 2)) / denom
    pair_flow = jnp.stack([flow_y, flow_x], 0)
    rows = lax.all_gather(pair_flow, "mesh", axis=1, tiled=True)
    linked = rows[:, node_links[0]]
    relaxed = 0.5 * linked[:, 0] + 0.5 * jnp.mean(linked[:, 1:], axis=1)
    return pair_flow, relaxed


def solution(mesh):
    split = ("parts", "tiles", "mesh")
    few = mesh.shape["tiles"] <= DIRECT_LIMIT
    return jax.shard_map(
        direct if few else general,
        mesh=mesh,
        in_specs=(P(split, None, None), P(split, None), P(split, None, None), P(split, None, None)),
        out_specs=(P(None, split), P(None, split)),
        check_vma=False,
    )
```

```python
import functools
import math

import jax
import jax.numpy as jnp
import numpy as np
from jax import lax
from jax.experimental import pallas as pl
from jax.experimental.pallas import tpu as pltpu
from jax.sharding import PartitionSpec as P


F32 = jnp.float32
BF16 = jnp.bfloat16
ANY = pl.BlockSpec(memory_space=pl.ANY)
SMEM = pl.BlockSpec(memory_space=pltpu.SMEM)
VMEM = pl.BlockSpec(memory_space=pltpu.VMEM)
DIRECT_LIMIT = 16


def const(array):
    return jnp.asarray(array.astype(np.float32)).astype(BF16)


def base_tables(side):
    ticks = np.arange(side)
    angle = 2.0 * np.pi / side * (ticks[:, None] * ticks[None, :] % side)
    cosine = np.cos(angle) / math.sqrt(side)
    sine = np.sin(angle) / math.sqrt(side)
    gap = (ticks[:, None] - ticks[None, :]).astype(np.float64)
    narrow = np.exp(-gap * gap / (2.0 * 0.35 * 0.35)) / (0.35 * math.sqrt(2.0 * math.pi))
    broad = np.exp(-gap * gap / 32.0) / (4.0 * math.sqrt(2.0 * math.pi))
    return cosine, sine, narrow - broad


def make_tables(side):
    cosine, sine, band = base_tables(side)
    left = np.concatenate([cosine, sine], 0)
    right = np.concatenate([cosine, sine], 1)
    back = np.concatenate([cosine, -sine], 1)
    return const(band), const(left), const(right), const(back)


def half_rows(side):
    return -(-(side // 2 + 1) // 16) * 16


def half_tables(side):
    cosine, sine, band = base_tables(side)
    half, rows = side // 2, half_rows(side)
    zero = np.zeros((side, side))
    band_pair = np.block([[band.T, zero], [zero, band.T]])
    left = np.zeros((2 * rows, side))
    left[: half + 1] = cosine[: half + 1]
    left[rows : rows + half + 1] = sine[: half + 1]
    forward = np.block([[cosine, -sine], [-sine, -cosine]])
    mixer = np.block([[cosine, sine], [-sine, cosine]])
    back = np.concatenate([2.0 * cosine[:, :half], -2.0 * sine[:, :half]], 1)
    back[:, 0] = cosine[:, 0]
    back[:, half] = cosine[:, half]
    return tuple(const(t) for t in (band, band_pair, left, forward, mixer, back))


def dot(a, b):
    return jnp.dot(a, b, preferred_element_type=F32)


def lag_of(shape, dim, side):
    place = lax.broadcasted_iota(jnp.int32, shape, dim).astype(F32)
    return jnp.where(place < side / 2, place, place - side)


GROUP = 4


def offsets(count):
    if count == 8:
        return [4, 5, 2, 3, 1, 6, 7]
    return list(range(count - 1, 0, -1))


def pick_kernel(order, cap, send_ref, patches_ref, *rest):
    outs, sems = rest[:-1], rest[-1]
    me = lax.axis_index("tiles")
    limit = patches_ref.shape[0]
    copies = []
    for k, d in enumerate(order):
        peer = me ^ d
        for s in range(cap):
            index = send_ref[0, peer * cap + s]
            copy = pltpu.make_async_copy(
                patches_ref.at[jnp.minimum(index, limit - 1)], outs[k].at[s], sems.at[k * cap + s]
            )
            copy.start()
            copies.append(copy)
    for copy in copies:
        copy.wait()
    for k, d in enumerate(order):
        peer = me ^ d
        for s in range(cap):

            @pl.when(send_ref[0, peer * cap + s] >= limit)
            def _():
                outs[k][s] = jnp.zeros(outs[k].shape[1:], outs[k].dtype)


def pick(patches, send_index, order, cap):
    side = patches.shape[-1]
    return pl.pallas_call(
        functools.partial(pick_kernel, order, cap),
        out_shape=[pltpu.VMEM((cap, side, side), patches.dtype)] * len(order),
        in_specs=[SMEM, ANY],
        out_specs=[VMEM] * len(order),
        scratch_shapes=[pltpu.SemaphoreType.DMA((len(order) * cap,))],
        name="pick",
    )(send_index, patches)


def spectra(x, band, band_pair, left, forward):
    side = x[0].shape[-1]
    rows = left.shape[0] // 2
    beside = []
    for k in range(0, len(x), 2):
        both = jnp.concatenate([x[k], x[k + 1]], 1)
        partial = dot(band, both).astype(BF16)
        filtered = dot(partial, band_pair).astype(BF16)
        halves = dot(left, filtered).astype(BF16)
        for at in (slice(0, side), slice(side, 2 * side)):
            beside.append(jnp.concatenate([halves[:rows, at], halves[rows:, at]], 1))
    whole = dot(jnp.concatenate(beside, 0), forward)
    return [whole[k * rows : (k + 1) * rows] for k in range(len(x))]


def flows_of(sides, signs, mixer, back):
    rows, side = sides[0][0].shape[0], back.shape[0]
    half = side // 2
    powers = []
    for (moving, fixed), sign in zip(sides, signs):
        mr, mi, fr, fi = moving[:, :side], moving[:, side:], fixed[:, :side], fixed[:, side:]
        imag = mi * fr - mr * fi
        powers.append(
            jnp.concatenate([mr * fr + mi * fi, imag if sign is None else imag * sign], 1).astype(BF16)
        )
    mixed = dot(jnp.concatenate(powers, 0), mixer)
    top = lax.broadcasted_iota(jnp.int32, (8, side), 0) == 0
    stacks = []
    for k in range(len(sides)):
        one = mixed[k * rows : (k + 1) * rows]
        first, second = one[:, :side], one[:, side:]
        swap = jnp.where(top, first[half : half + 8], second[:8])
        stacks.append(jnp.concatenate([first[:half], swap, second[8:half]], 0).astype(BF16))
    lag = lag_of((side, side), 0, side)
    plain, by_row = [], []
    for k in range(0, len(sides), 2):
        surface = dot(back, jnp.concatenate([stacks[k], stacks[k + 1]], 1))
        for at in (slice(0, side), slice(side, 2 * side)):
            weight = surface[:, at] * surface[:, at]
            plain.append(jnp.sum(weight, 0, keepdims=True))
            by_row.append(jnp.sum(lag * weight, 0, keepdims=True))
    plain = jnp.concatenate(plain, 0)
    by_row = jnp.concatenate(by_row, 0)
    scale = 1.0 / (side * side)
    denom = jnp.sum(plain, 1, keepdims=True) * scale + 1e-06
    flow_y = jnp.sum(by_row, 1, keepdims=True) * scale / denom
    flow_x = jnp.sum(plain * lag_of(plain.shape, 1, side), 1, keepdims=True) * scale / denom
    return flow_y, flow_x


def first_kernel(
    order, cap, slots_ref, links_ref, x, band, band_pair, left, forward,
    spec, mix_ref, place_ref, meta_ref, base_ref,
):
    count = len(order)
    total = count * cap
    pairs = slots_ref.shape[-1]
    shift = cap.bit_length() - 1
    me = lax.axis_index("tiles")

    for source in range(count):
        off = me ^ source
        at = jnp.int32(0)
        for k, d in enumerate(order):
            at = jnp.where(off == d, k * cap, at)
        base_ref[source] = at
    base_ref[count] = total
    for s in range(cap + 1):
        meta_ref[0, s] = -1
        meta_ref[1, s] = 0
        meta_ref[2, s] = total
    late = (count - 1) * cap
    for q in range(pairs):
        a, b = slots_ref[0, 0, q], slots_ref[0, 1, q]
        a = base_ref[a >> shift] + (a & (cap - 1))
        b = base_ref[b >> shift] + (b & (cap - 1))
        place_ref[0, q] = a
        place_ref[1, q] = b
        at = jnp.where((a >= late) & (a < total), a - late, cap)
        meta_ref[0, at] = q
        meta_ref[1, at] = 1
        meta_ref[2, at] = b
        at = jnp.where((b >= late) & (b < total), b - late, cap)
        meta_ref[0, at] = q
        meta_ref[1, at] = -1
        meta_ref[2, at] = a

    row = lax.broadcasted_iota(jnp.int32, mix_ref.shape, 0)
    links = links_ref.shape[1]
    mix = jnp.zeros(mix_ref.shape, F32)
    for k in range(links):
        share = 0.5 if k == 0 else 0.5 / (links - 1)
        mix += jnp.where(row == links_ref[0, k : k + 1, :], share, 0.0)
    mix_ref[...] = mix

    spec[late:] = jnp.zeros((spec.shape[0] - late,) + spec.shape[1:], F32)
    sides = [x[s] for s in range(cap)]
    for s, one in enumerate(spectra(sides, band[...], band_pair[...], left[...], forward[...])):
        spec[s] = one


def next_kernel(start, *refs):
    spec_in, band, band_pair, left, forward = refs[:5]
    chunks, spec = refs[5:-1], refs[-1]
    cap = chunks[0].shape[0]
    for k, x in enumerate(chunks):
        sides = [x[s] for s in range(cap)]
        for s, one in enumerate(spectra(sides, band[...], band_pair[...], left[...], forward[...])):
            spec[(start + k) * cap + s] = one


def early_kernel(spec, place_ref, meta_ref, mixer, back, flow_ref, other_ref):
    pairs = place_ref.shape[-1]
    cap = other_ref.shape[0]
    side = back.shape[0]

    @pl.loop(0, pairs // GROUP)
    def _(g):
        sides = [
            (spec[place_ref[0, g * GROUP + j]], spec[place_ref[1, g * GROUP + j]])
            for j in range(GROUP)
        ]
        flow_y, flow_x = flows_of(sides, [None] * GROUP, mixer[...], back[...])
        for j in range(GROUP):
            at = pl.ds(g * GROUP + j, 1)
            flow_ref[0, at] = jnp.broadcast_to(flow_y[j : j + 1], (1, side))
            flow_ref[1, at] = jnp.broadcast_to(flow_x[j : j + 1], (1, side))

    for s in range(cap):
        other_ref[s] = spec[meta_ref[2, s]]


def last_kernel(
    x, flow_in, other, meta_ref, band, band_pair, left, forward, mixer, back, flow_ref, pair_ref
):
    cap, side = x.shape[0], x.shape[-1]
    pairs = flow_in.shape[1]
    sides = [x[s] for s in range(cap)]
    own = spectra(sides, band[...], band_pair[...], left[...], forward[...])
    signs = [meta_ref[1, s].astype(F32) for s in range(cap)]
    flow_y, flow_x = flows_of(
        [(own[s], other[s]) for s in range(cap)], signs, mixer[...], back[...]
    )
    row = lax.broadcasted_iota(jnp.int32, (pairs, side), 0)
    diagonal = row == lax.broadcasted_iota(jnp.int32, (pairs, side), 1)
    for c, late in enumerate((flow_y, flow_x)):
        out = flow_in[c]
        for s in range(cap):
            out = jnp.where(row == meta_ref[0, s], late[s : s + 1], out)
        flow_ref[c] = out
        line = jnp.sum(jnp.where(diagonal, out, 0.0), 0, keepdims=True)
        pair_ref[c : c + 1] = line[:, :pairs]


def relax_kernel(flow_ref, mix_ref, out_ref):
    mix = mix_ref[...]
    for c in range(2):
        flow = jnp.concatenate([flow_ref[m, c] for m in range(flow_ref.shape[0])], 0)
        out_ref[c : c + 1] = jnp.sum(flow * mix, 0, keepdims=True)


def near(x):
    return pltpu.with_memory_space_constraint(x, pltpu.VMEM)


def near_scalars(x):
    return pltpu.with_memory_space_constraint(x, pltpu.SMEM)


def direct(patches, send_index, pair_slots, node_links):
    side = patches.shape[-1]
    pairs = pair_slots.shape[-1]
    nodes = node_links.shape[-1]
    count = lax.axis_size("tiles")
    meshes = lax.axis_size("mesh")
    cap = send_index.shape[-1] // count
    order = [0] + offsets(count)
    total = count * cap
    rows = half_rows(side)
    tables = half_tables(side)
    ahead, behind = tables[:4], tables[4:]
    picked = pick(patches, send_index, order, cap)
    chunks = [picked[0]]
    for k in range(1, count):
        path = [(i, i ^ order[k]) for i in range(count)]
        chunks.append(lax.ppermute(picked[k], "tiles", path))

    spec_shape = pltpu.VMEM((total + 1, rows, 2 * side), F32)
    spec, mix, place, meta = pl.pallas_call(
        functools.partial(first_kernel, order, cap),
        out_shape=[
            spec_shape,
            pltpu.VMEM((meshes * pairs, nodes), F32),
            pltpu.SMEM((2, pairs), jnp.int32),
            pltpu.SMEM((3, cap + 1), jnp.int32),
        ],
        in_specs=[SMEM] + [VMEM] * 6,
        out_specs=[VMEM, VMEM, SMEM, SMEM],
        scratch_shapes=[pltpu.SMEM((count + 1,), jnp.int32)],
        name="first",
    )(pair_slots, node_links, near(chunks[0]), *ahead)
    for start, stop in ((1, 3), (3, 6), (6, count - 1)):
        if start >= stop:
            continue
        spec = pl.pallas_call(
            functools.partial(next_kernel, start),
            out_shape=spec_shape,
            in_specs=[VMEM] * (5 + stop - start),
            out_specs=VMEM,
            input_output_aliases={0: 0},
            name=f"next{start}",
        )(near(spec), *ahead, *(near(c) for c in chunks[start:stop]))
    flow, other = pl.pallas_call(
        early_kernel,
        out_shape=[
            pltpu.VMEM((2, pairs, side), F32),
            pltpu.VMEM((cap, rows, 2 * side), F32),
        ],
        in_specs=[VMEM, SMEM, SMEM, VMEM, VMEM],
        out_specs=[VMEM, VMEM],
        name="early",
    )(near(spec), near_scalars(place), near_scalars(meta), *behind)
    flow, pair_flow = pl.pallas_call(
        last_kernel,
        out_shape=[
            pltpu.VMEM((2, pairs, side), F32),
            jax.ShapeDtypeStruct((2, pairs), F32),
        ],
        in_specs=[VMEM, VMEM, VMEM, SMEM] + [VMEM] * 6,
        out_specs=[VMEM, VMEM],
        name="last",
    )(near(chunks[-1]), near(flow), near(other), near_scalars(meta), *(near(t) for t in tables))
    both = lax.all_gather(flow, "mesh")
    relaxed = pl.pallas_call(
        relax_kernel,
        out_shape=jax.ShapeDtypeStruct((2, nodes), F32),
        in_specs=[VMEM, VMEM],
        out_specs=VMEM,
        name="relax",
    )(near(both), near(mix))
    return pair_flow, relaxed


def general(patches, send_index, pair_slots, node_links):
    side = patches.shape[-1]
    held = patches.shape[0]
    pairs = pair_slots.shape[-1]
    count = lax.axis_size("tiles")
    band, left, right, back = make_tables(side)
    wanted = send_index[0]
    cap = wanted.shape[0] // count
    picked = patches[jnp.minimum(wanted, held - 1)]
    picked = jnp.where((wanted < held)[:, None, None], picked, jnp.zeros_like(picked))
    received = lax.all_to_all(
        picked.reshape((count, cap) + patches.shape[1:]), "tiles", 0, 0, tiled=True
    )
    total = count * cap
    received = received.reshape((total,) + received.shape[2:])
    slots = pair_slots[0].reshape(-1)
    chosen = received[jnp.minimum(slots, total - 1)]
    chosen = jnp.where((slots < total)[:, None, None], chosen, jnp.zeros_like(chosen))

    def mul(form, a, b):
        return jnp.einsum(form, a, b, preferred_element_type=F32)

    partial = mul("ij,bjk->bik", band, chosen).astype(BF16)
    filtered = mul("bij,kj->bik", partial, band).astype(BF16)
    halves = mul("ij,bjk->bik", left, filtered).astype(BF16)
    quarter = mul("bij,jk->bik", halves, right)
    real = quarter[:, :side, :side] - quarter[:, side:, side:]
    imag = -(quarter[:, :side, side:] + quarter[:, side:, :side])
    mr, fr, mi, fi = real[:pairs], real[pairs:], imag[:pairs], imag[pairs:]
    power = jnp.concatenate([mr * fr + mi * fi, mi * fr - mr * fi], 1).astype(BF16)
    mixed = mul("bij,jk->bik", power, right)
    first = mixed[:, :side, :side] - mixed[:, side:, side:]
    second = mixed[:, :side, side:] + mixed[:, side:, :side]
    stacked = jnp.concatenate([first, second], 1).astype(BF16)
    weight = mul("ij,bjk->bik", back, stacked) ** 2
    lag = jnp.asarray(np.where(np.arange(side) < side / 2, 0, -side) + np.arange(side), F32)
    denom = jnp.mean(weight, axis=(1, 2)) + 1e-06
    flow_y = jnp.mean(lag[None, :, None] * weight, axis=(1, 2)) / denom
    flow_x = jnp.mean(lag[None, None, :] * weight, axis=(1, 2)) / denom
    pair_flow = jnp.stack([flow_y, flow_x], 0)
    rows = lax.all_gather(pair_flow, "mesh", axis=1, tiled=True)
    linked = rows[:, node_links[0]]
    relaxed = 0.5 * linked[:, 0] + 0.5 * jnp.mean(linked[:, 1:], axis=1)
    return pair_flow, relaxed

def per_device(patches, send_index, pair_slots, node_links):
    count = lax.axis_size("tiles")
    cap = send_index.shape[-1] // count
    pairs = pair_slots.shape[-1]
    few = 2 < count <= DIRECT_LIMIT and count & (count - 1) == 0
    if few and cap % 2 == 0 and cap & (cap - 1) == 0 and pairs % GROUP == 0:
        return direct(patches, send_index, pair_slots, node_links)
    return general(patches, send_index, pair_slots, node_links)


def solution(mesh):
    split = ("parts", "tiles", "mesh")
    return jax.shard_map(
        per_device,
        mesh=mesh,
        in_specs=(P(split, None, None), P(split, None), P(split, None, None), P(split, None, None)),
        out_specs=(P(None, split), P(None, split)),
        check_vma=False,
    )
```

```python
import functools
import math

import jax
import jax.numpy as jnp
import numpy as np
from jax import lax
from jax.experimental import pallas as pl
from jax.experimental.pallas import tpu as pltpu
from jax.sharding import PartitionSpec as P


F32 = jnp.float32
BF16 = jnp.bfloat16
ANY = pl.BlockSpec(memory_space=pl.ANY)
SMEM = pl.BlockSpec(memory_space=pltpu.SMEM)
VMEM = pl.BlockSpec(memory_space=pltpu.VMEM)
DIRECT_LIMIT = 16


def const(array):
    return jnp.asarray(array.astype(np.float32)).astype(BF16)


def base_tables(side):
    ticks = np.arange(side)
    angle = 2.0 * np.pi / side * (ticks[:, None] * ticks[None, :] % side)
    cosine = np.cos(angle) / math.sqrt(side)
    sine = np.sin(angle) / math.sqrt(side)
    gap = (ticks[:, None] - ticks[None, :]).astype(np.float64)
    narrow = np.exp(-gap * gap / (2.0 * 0.35 * 0.35)) / (0.35 * math.sqrt(2.0 * math.pi))
    broad = np.exp(-gap * gap / 32.0) / (4.0 * math.sqrt(2.0 * math.pi))
    return cosine, sine, narrow - broad


def make_tables(side):
    cosine, sine, band = base_tables(side)
    left = np.concatenate([cosine, sine], 0)
    right = np.concatenate([cosine, sine], 1)
    back = np.concatenate([cosine, -sine], 1)
    return const(band), const(left), const(right), const(back)


def half_rows(side):
    return -(-(side // 2 + 1) // 16) * 16


def half_tables(side):
    cosine, sine, band = base_tables(side)
    half, rows = side // 2, half_rows(side)
    zero = np.zeros((side, side))
    band_pair = np.block([[band.T, zero], [zero, band.T]])
    left = np.zeros((2 * rows, side))
    left[: half + 1] = cosine[: half + 1]
    left[rows : rows + half + 1] = sine[: half + 1]
    forward = np.block([[cosine, -sine], [-sine, -cosine]])
    mixer = np.block([[cosine, sine], [-sine, cosine]])
    back = np.concatenate([2.0 * cosine[:, :half], -2.0 * sine[:, :half]], 1)
    back[:, 0] = cosine[:, 0]
    back[:, half] = cosine[:, half]
    small = np.concatenate([band, back], 1)
    left = np.concatenate([left, np.zeros_like(left)], 1)
    return const(np.concatenate([band_pair, forward, mixer, small, left], 0))


def split_table(table):
    side = table.shape[-1] // 2
    forward, mixer, small, left = 2 * side, 4 * side, 6 * side, 7 * side
    return (
        table[small:left, :side],
        table[:forward, :],
        table[left:, :side],
        table[forward:mixer, :],
        table[mixer:small, :],
        table[small:left, side:],
    )


def dot(a, b):
    return jnp.dot(a, b, preferred_element_type=F32)


def lag_of(shape, dim, side):
    place = lax.broadcasted_iota(jnp.int32, shape, dim).astype(F32)
    return jnp.where(place < side / 2, place, place - side)


GROUP = 4
STAGES = ((1, 3), (3, 6))
PARAMS = pltpu.CompilerParams(vmem_limit_bytes=8 * 2**20)


def offsets(count):
    if count == 8:
        return [4, 5, 2, 3, 1, 6, 7]
    return list(range(count - 1, 0, -1))


def pick_kernel(order, cap, send_ref, patches_ref, *rest):
    outs, sems = rest[:-1], rest[-1]
    me = lax.axis_index("tiles")
    limit = patches_ref.shape[0]
    copies = []
    for k, d in enumerate(order):
        peer = me ^ d
        for s in range(cap):
            index = send_ref[0, peer * cap + s]
            copy = pltpu.make_async_copy(
                patches_ref.at[jnp.minimum(index, limit - 1)], outs[k].at[s], sems.at[k * cap + s]
            )
            copy.start()
            copies.append(copy)
    for copy in copies:
        copy.wait()
    for k, d in enumerate(order):
        peer = me ^ d
        for s in range(cap):

            @pl.when(send_ref[0, peer * cap + s] >= limit)
            def _():
                outs[k][s] = jnp.zeros(outs[k].shape[1:], outs[k].dtype)


def pick(patches, send_index, order, cap):
    side = patches.shape[-1]
    return pl.pallas_call(
        functools.partial(pick_kernel, order, cap),
        out_shape=[pltpu.VMEM((cap, side, side), patches.dtype)] * len(order),
        in_specs=[SMEM, ANY],
        out_specs=[VMEM] * len(order),
        scratch_shapes=[pltpu.SemaphoreType.DMA((len(order) * cap,))],
        compiler_params=PARAMS,
        name="pick",
    )(far(send_index), far(patches))


def spectra(x, band, band_pair, left, forward):
    side = x[0].shape[-1]
    rows = left.shape[0] // 2
    beside = []
    for k in range(0, len(x), 2):
        both = jnp.concatenate([x[k], x[k + 1]], 1)
        partial = dot(band, both).astype(BF16)
        filtered = dot(partial, band_pair).astype(BF16)
        halves = dot(left, filtered).astype(BF16)
        for at in (slice(0, side), slice(side, 2 * side)):
            beside.append(jnp.concatenate([halves[:rows, at], halves[rows:, at]], 1))
    whole = dot(jnp.concatenate(beside, 0), forward)
    return [whole[k * rows : (k + 1) * rows] for k in range(len(x))]


def flows_of(sides, signs, mixer, back):
    rows, side = sides[0][0].shape[0], back.shape[0]
    half = side // 2
    powers = []
    for (moving, fixed), sign in zip(sides, signs):
        mr, mi, fr, fi = moving[:, :side], moving[:, side:], fixed[:, :side], fixed[:, side:]
        imag = mi * fr - mr * fi
        powers.append(
            jnp.concatenate([mr * fr + mi * fi, imag if sign is None else imag * sign], 1).astype(BF16)
        )
    mixed = dot(jnp.concatenate(powers, 0), mixer)
    top = lax.broadcasted_iota(jnp.int32, (8, side), 0) == 0
    stacks = []
    for k in range(len(sides)):
        one = mixed[k * rows : (k + 1) * rows]
        first, second = one[:, :side], one[:, side:]
        swap = jnp.where(top, first[half : half + 8], second[:8])
        stacks.append(jnp.concatenate([first[:half], swap, second[8:half]], 0).astype(BF16))
    lag = lag_of((side, side), 0, side)
    plain, by_row = [], []
    for k in range(0, len(sides), 2):
        surface = dot(back, jnp.concatenate([stacks[k], stacks[k + 1]], 1))
        for at in (slice(0, side), slice(side, 2 * side)):
            weight = surface[:, at] * surface[:, at]
            plain.append(jnp.sum(weight, 0, keepdims=True))
            by_row.append(jnp.sum(lag * weight, 0, keepdims=True))
    plain = jnp.concatenate(plain, 0)
    by_row = jnp.concatenate(by_row, 0)
    scale = 1.0 / (side * side)
    denom = jnp.sum(plain, 1, keepdims=True) * scale + 1e-06
    flow_y = jnp.sum(by_row, 1, keepdims=True) * scale / denom
    flow_x = jnp.sum(plain * lag_of(plain.shape, 1, side), 1, keepdims=True) * scale / denom
    return flow_y, flow_x


def first_kernel(
    order, cap, slots_ref, links_ref, x, far_table,
    spec, mix_ref, place_ref, meta_ref, table, base_ref, sem,
):
    copy = pltpu.make_async_copy(far_table, table, sem)
    copy.start()
    count = len(order)
    total = count * cap
    pairs = slots_ref.shape[-1]
    shift = cap.bit_length() - 1
    me = lax.axis_index("tiles")

    for source in range(count):
        off = me ^ source
        at = jnp.int32(0)
        for k, d in enumerate(order):
            at = jnp.where(off == d, k * cap, at)
        base_ref[source] = at
    base_ref[count] = total
    for s in range(cap + 1):
        meta_ref[0, s] = -1
        meta_ref[1, s] = 0
        meta_ref[2, s] = total
    late = (count - 1) * cap
    for q in range(pairs):
        a, b = slots_ref[0, 0, q], slots_ref[0, 1, q]
        a = base_ref[a >> shift] + (a & (cap - 1))
        b = base_ref[b >> shift] + (b & (cap - 1))
        place_ref[0, q] = a
        place_ref[1, q] = b
        at = jnp.where((a >= late) & (a < total), a - late, cap)
        meta_ref[0, at] = q
        meta_ref[1, at] = 1
        meta_ref[2, at] = b
        at = jnp.where((b >= late) & (b < total), b - late, cap)
        meta_ref[0, at] = q
        meta_ref[1, at] = -1
        meta_ref[2, at] = a

    row = lax.broadcasted_iota(jnp.int32, mix_ref.shape, 0)
    links = links_ref.shape[1]
    mix = jnp.zeros(mix_ref.shape, F32)
    for k in range(links):
        share = 0.5 if k == 0 else 0.5 / (links - 1)
        mix += jnp.where(row == links_ref[0, k : k + 1, :], share, 0.0)
    mix_ref[...] = mix

    spec[late:] = jnp.zeros((spec.shape[0] - late,) + spec.shape[1:], F32)
    copy.wait()
    fill(spec, 0, x, table)


def fill(spec, start, x, table):
    cap = x.shape[0]
    for s, one in enumerate(spectra([x[s] for s in range(cap)], *split_table(table)[:4])):
        spec[start * cap + s] = one


def next_kernel(start, *refs):
    table, chunks, spec = refs[1], refs[2:-1], refs[-1]
    for k, x in enumerate(chunks):
        fill(spec, start + k, x, table)


def early_kernel(
    start, spec_in, table, place_ref, meta_ref, x, spec, flow_ref, other_ref
):
    pairs = place_ref.shape[-1]
    cap = other_ref.shape[0]
    tables = split_table(table)
    side = tables[0].shape[0]
    fill(spec, start, x, table)

    @pl.loop(0, pairs // GROUP)
    def _(g):
        sides = [
            (spec[place_ref[0, g * GROUP + j]], spec[place_ref[1, g * GROUP + j]])
            for j in range(GROUP)
        ]
        mixer, back = split_table(table)[4:]
        flow_y, flow_x = flows_of(sides, [None] * GROUP, mixer, back)
        for j in range(GROUP):
            at = pl.ds(g * GROUP + j, 1)
            flow_ref[0, at] = jnp.broadcast_to(flow_y[j : j + 1], (1, side))
            flow_ref[1, at] = jnp.broadcast_to(flow_x[j : j + 1], (1, side))

    for s in range(cap):
        other_ref[s] = spec[meta_ref[2, s]]


def last_kernel(x, flow_in, other, meta_ref, table, flow_ref, pair_ref):
    cap, side = x.shape[0], x.shape[-1]
    pairs = flow_in.shape[1]
    tables = split_table(table)
    own = spectra([x[s] for s in range(cap)], *tables[:4])
    signs = [meta_ref[1, s].astype(F32) for s in range(cap)]
    flow_y, flow_x = flows_of([(own[s], other[s]) for s in range(cap)], signs, *tables[4:])
    row = lax.broadcasted_iota(jnp.int32, (pairs, side), 0)
    diagonal = row == lax.broadcasted_iota(jnp.int32, (pairs, side), 1)
    for c, late in enumerate((flow_y, flow_x)):
        out = flow_in[c]
        for s in range(cap):
            out = jnp.where(row == meta_ref[0, s], late[s : s + 1], out)
        flow_ref[c] = out
        line = jnp.sum(jnp.where(diagonal, out, 0.0), 0, keepdims=True)
        pair_ref[c : c + 1] = line[:, :pairs]


def relax_kernel(flow_ref, mix_ref, out_ref):
    mix = mix_ref[...]
    for c in range(2):
        flow = jnp.concatenate([flow_ref[m, c] for m in range(flow_ref.shape[0])], 0)
        out_ref[c : c + 1] = jnp.sum(flow * mix, 0, keepdims=True)


def near(x):
    return pltpu.with_memory_space_constraint(x, pltpu.VMEM)


def far(x):
    return pltpu.with_memory_space_constraint(x, pltpu.HBM)


def near_scalars(x):
    return pltpu.with_memory_space_constraint(x, pltpu.SMEM)


def direct(patches, send_index, pair_slots, node_links):
    side = patches.shape[-1]
    pairs = pair_slots.shape[-1]
    nodes = node_links.shape[-1]
    count = lax.axis_size("tiles")
    meshes = lax.axis_size("mesh")
    cap = send_index.shape[-1] // count
    order = [0] + offsets(count)
    total = count * cap
    rows = half_rows(side)
    table = half_tables(side)
    picked = pick(patches, send_index, order, cap)
    chunks = [near(picked[0])]
    for k in range(1, count):
        path = [(i, i ^ order[k]) for i in range(count)]
        chunks.append(near(lax.ppermute(picked[k], "tiles", path)))

    spec_shape = pltpu.VMEM((total + 1, rows, 2 * side), F32)
    spec, mix, place, meta, table = pl.pallas_call(
        functools.partial(first_kernel, order, cap),
        out_shape=[
            spec_shape,
            pltpu.VMEM((meshes * pairs, nodes), F32),
            pltpu.SMEM((2, pairs), jnp.int32),
            pltpu.SMEM((3, cap + 1), jnp.int32),
            pltpu.VMEM(table.shape, table.dtype),
        ],
        in_specs=[SMEM, VMEM, VMEM, ANY],
        out_specs=[VMEM, VMEM, SMEM, SMEM, VMEM],
        scratch_shapes=[pltpu.SMEM((count + 1,), jnp.int32), pltpu.SemaphoreType.DMA],
        compiler_params=PARAMS,
        name="first",
    )(far(pair_slots), far(node_links), chunks[0], far(table))
    table = near(table)
    place, meta = near_scalars(place), near_scalars(meta)
    for start, stop in STAGES if count == 8 else ((1, count - 2),):
        if start >= stop:
            continue
        spec = pl.pallas_call(
            functools.partial(next_kernel, start),
            out_shape=spec_shape,
            in_specs=[VMEM] * (2 + stop - start),
            out_specs=VMEM,
            input_output_aliases={0: 0},
            compiler_params=PARAMS,
            name=f"next{start}",
        )(near(spec), table, *chunks[start:stop])
    spec, flow, other = pl.pallas_call(
        functools.partial(early_kernel, count - 2),
        out_shape=[
            spec_shape,
            pltpu.VMEM((2, pairs, side), F32),
            pltpu.VMEM((cap, rows, 2 * side), F32),
        ],
        in_specs=[VMEM, VMEM, SMEM, SMEM, VMEM],
        out_specs=[VMEM, VMEM, VMEM],
        input_output_aliases={0: 0},
        compiler_params=PARAMS,
        name="early",
    )(near(spec), table, place, meta, chunks[-2])
    flow, pair_flow = pl.pallas_call(
        last_kernel,
        out_shape=[
            pltpu.VMEM((2, pairs, side), F32),
            jax.ShapeDtypeStruct((2, pairs), F32),
        ],
        in_specs=[VMEM, VMEM, VMEM, SMEM, VMEM],
        out_specs=[VMEM, VMEM],
        compiler_params=PARAMS,
        name="last",
    )(chunks[-1], near(flow), near(other), meta, table)
    both = lax.all_gather(flow, "mesh")
    relaxed = pl.pallas_call(
        relax_kernel,
        out_shape=jax.ShapeDtypeStruct((2, nodes), F32),
        in_specs=[VMEM, VMEM],
        out_specs=VMEM,
        compiler_params=PARAMS,
        name="relax",
    )(near(both), near(mix))
    return pair_flow, relaxed


def general(patches, send_index, pair_slots, node_links):
    side = patches.shape[-1]
    held = patches.shape[0]
    pairs = pair_slots.shape[-1]
    count = lax.axis_size("tiles")
    band, left, right, back = make_tables(side)
    wanted = send_index[0]
    cap = wanted.shape[0] // count
    picked = patches[jnp.minimum(wanted, held - 1)]
    picked = jnp.where((wanted < held)[:, None, None], picked, jnp.zeros_like(picked))
    received = lax.all_to_all(
        picked.reshape((count, cap) + patches.shape[1:]), "tiles", 0, 0, tiled=True
    )
    total = count * cap
    received = received.reshape((total,) + received.shape[2:])
    slots = pair_slots[0].reshape(-1)
    chosen = received[jnp.minimum(slots, total - 1)]
    chosen = jnp.where((slots < total)[:, None, None], chosen, jnp.zeros_like(chosen))

    def mul(form, a, b):
        return jnp.einsum(form, a, b, preferred_element_type=F32)

    partial = mul("ij,bjk->bik", band, chosen).astype(BF16)
    filtered = mul("bij,kj->bik", partial, band).astype(BF16)
    halves = mul("ij,bjk->bik", left, filtered).astype(BF16)
    quarter = mul("bij,jk->bik", halves, right)
    real = quarter[:, :side, :side] - quarter[:, side:, side:]
    imag = -(quarter[:, :side, side:] + quarter[:, side:, :side])
    mr, fr, mi, fi = real[:pairs], real[pairs:], imag[:pairs], imag[pairs:]
    power = jnp.concatenate([mr * fr + mi * fi, mi * fr - mr * fi], 1).astype(BF16)
    mixed = mul("bij,jk->bik", power, right)
    first = mixed[:, :side, :side] - mixed[:, side:, side:]
    second = mixed[:, :side, side:] + mixed[:, side:, :side]
    stacked = jnp.concatenate([first, second], 1).astype(BF16)
    weight = mul("ij,bjk->bik", back, stacked) ** 2
    lag = jnp.asarray(np.where(np.arange(side) < side / 2, 0, -side) + np.arange(side), F32)
    denom = jnp.mean(weight, axis=(1, 2)) + 1e-06
    flow_y = jnp.mean(lag[None, :, None] * weight, axis=(1, 2)) / denom
    flow_x = jnp.mean(lag[None, None, :] * weight, axis=(1, 2)) / denom
    pair_flow = jnp.stack([flow_y, flow_x], 0)
    rows = lax.all_gather(pair_flow, "mesh", axis=1, tiled=True)
    linked = rows[:, node_links[0]]
    relaxed = 0.5 * linked[:, 0] + 0.5 * jnp.mean(linked[:, 1:], axis=1)
    return pair_flow, relaxed

def per_device(patches, send_index, pair_slots, node_links):
    count = lax.axis_size("tiles")
    cap = send_index.shape[-1] // count
    pairs = pair_slots.shape[-1]
    few = 2 < count <= DIRECT_LIMIT and count & (count - 1) == 0
    if few and cap % 2 == 0 and cap & (cap - 1) == 0 and pairs % GROUP == 0:
        return direct(patches, send_index, pair_slots, node_links)
    return general(patches, send_index, pair_slots, node_links)


def solution(mesh):
    split = ("parts", "tiles", "mesh")
    return jax.shard_map(
        per_device,
        mesh=mesh,
        in_specs=(P(split, None, None), P(split, None), P(split, None, None), P(split, None, None)),
        out_specs=(P(None, split), P(None, split)),
        check_vma=False,
    )
```

```python
import functools
import math

import jax
import jax.numpy as jnp
import numpy as np
from jax import lax
from jax.experimental import pallas as pl
from jax.experimental.pallas import tpu as pltpu
from jax.sharding import PartitionSpec as P


F32 = jnp.float32
BF16 = jnp.bfloat16
ANY = pl.BlockSpec(memory_space=pl.ANY)
SMEM = pl.BlockSpec(memory_space=pltpu.SMEM)
VMEM = pl.BlockSpec(memory_space=pltpu.VMEM)
DIRECT_LIMIT = 16


def const(array):
    return jnp.asarray(array.astype(np.float32)).astype(BF16)


def base_tables(side):
    ticks = np.arange(side)
    angle = 2.0 * np.pi / side * (ticks[:, None] * ticks[None, :] % side)
    cosine = np.cos(angle) / math.sqrt(side)
    sine = np.sin(angle) / math.sqrt(side)
    gap = (ticks[:, None] - ticks[None, :]).astype(np.float64)
    narrow = np.exp(-gap * gap / (2.0 * 0.35 * 0.35)) / (0.35 * math.sqrt(2.0 * math.pi))
    broad = np.exp(-gap * gap / 32.0) / (4.0 * math.sqrt(2.0 * math.pi))
    return cosine, sine, narrow - broad


def make_tables(side):
    cosine, sine, band = base_tables(side)
    left = np.concatenate([cosine, sine], 0)
    right = np.concatenate([cosine, sine], 1)
    back = np.concatenate([cosine, -sine], 1)
    return const(band), const(left), const(right), const(back)


def half_rows(side):
    return -(-(side // 2 + 1) // 16) * 16


def half_tables(side):
    cosine, sine, band = base_tables(side)
    half = side // 2
    zero = np.zeros((side, side))
    band_pair = np.block([[band.T, zero], [zero, band.T]])
    left = np.concatenate([cosine[: half + 1], sine[1:half]], 0)
    forward = np.block([[cosine, -sine], [-sine, -cosine]])
    mixer = np.block([[cosine, sine], [-sine, cosine]])
    back = np.concatenate([2.0 * cosine[:, :half], -2.0 * sine[:, :half]], 1)
    back[:, 0] = cosine[:, 0]
    back[:, half] = cosine[:, half]
    small = np.concatenate([band, back], 1)
    left = np.concatenate([left, zero], 1)
    return const(np.concatenate([band_pair, forward, mixer, small, left], 0))


def split_table(table):
    side = table.shape[-1] // 2
    forward, mixer, small, left = 2 * side, 4 * side, 6 * side, 7 * side
    return (
        table[small:left, :side],
        table[:forward, :],
        table[left:, :side],
        table[forward:mixer, :],
        table[mixer:small, :],
        table[small:left, side:],
    )


def dot(a, b):
    return jnp.dot(a, b, preferred_element_type=F32)


def lag_of(shape, dim, side):
    place = lax.broadcasted_iota(jnp.int32, shape, dim).astype(F32)
    return jnp.where(place < side / 2, place, place - side)


GROUP = 4
STAGES = ((1, 2), (2, 3), (3, 5))
PARAMS = pltpu.CompilerParams(vmem_limit_bytes=8 * 2**20)


MODE = "xor"


def offsets(count):
    if count == 8:
        return [4, 5, 2, 3, 1, 6, 7]
    return list(range(count - 1, 0, -1))


def target(me, d, count):
    if MODE == "xor":
        return me ^ d
    if MODE == "shift":
        return (me + d) & (count - 1)
    return ((((me >> 1) + (d >> 1)) & (count // 2 - 1)) << 1) + ((me ^ d) & 1)


def offset_from(source, me, count):
    if MODE == "xor":
        return me ^ source
    if MODE == "shift":
        return (me - source) & (count - 1)
    return ((((me >> 1) - (source >> 1)) & (count // 2 - 1)) << 1) + ((me ^ source) & 1)


def fetch(ranks, order, cap, send_ref, patches_ref, outs, sems):
    count = len(order)
    me = lax.axis_index("tiles")
    limit = patches_ref.shape[0]
    copies, indices = [], []
    for k, out in zip(ranks, outs):
        peer = target(me, order[k], count)
        for s in range(cap):
            index = send_ref[0, peer * cap + s]
            source = patches_ref.at[jnp.minimum(index, limit - 1)]
            copy = pltpu.make_async_copy(source, out.at[s], sems.at[len(copies)])
            copy.start()
            copies.append(copy)
            indices.append(index)

    def end():
        for copy in copies:
            copy.wait()
        most = functools.reduce(jnp.maximum, indices)

        @pl.when(most >= limit)
        def _():
            for n, index in enumerate(indices):
                keep = jnp.where(index < limit, 1.0, 0.0).astype(BF16)
                out = outs[n // cap]
                out[n % cap] = out[n % cap] * keep

    return end


def pick_first_kernel(order, cap, send_ref, patches_ref, out, sems):
    fetch([1], order, cap, send_ref, patches_ref, [out], sems)()


def pick_rest_kernel(order, cap, send_ref, patches_ref, far_table, *rest):
    count = len(order)
    outs, halves, table = rest[: count - 3], rest[count - 3 : count - 1], rest[count - 1]
    held, sems, sem = rest[count:]
    copy = pltpu.make_async_copy(far_table, table, sem)
    copy.start()
    ranks = [0] + list(range(2, count))
    places = list(outs) + [held.at[0], held.at[1]]
    end = fetch(ranks, order, cap, send_ref, patches_ref, places, sems)
    copy.wait()
    end()
    for n in range(2):
        for s, one in enumerate(halves_of([held[n, s] for s in range(cap)], *split_table(table)[:3])):
            halves[n][s] = one


def halves_of(x, band, band_pair, left):
    side = x[0].shape[-1]
    result = []
    for k in range(0, len(x), 2):
        both = jnp.concatenate([x[k], x[k + 1]], 1)
        partial = dot(band, both).astype(BF16)
        filtered = dot(partial, band_pair).astype(BF16)
        halves = dot(left, filtered).astype(BF16)
        result += [halves[:, :side], halves[:, side:]]
    return result


def spectra(halves, forward):
    side = halves[0].shape[-1]
    half, rows = side // 2, half_rows(side)
    top = lax.broadcasted_iota(jnp.int32, (16, side), 0) == 0
    nothing = jnp.zeros((rows - half, side), BF16)
    beside = []
    for one in halves:
        mixed = one[half : half + 16].astype(F32)
        middle = jnp.where(top, mixed, 0.0).astype(BF16)
        sines = jnp.where(top, 0.0, mixed).astype(BF16)
        if rows - half > 16:
            middle = jnp.concatenate([middle, nothing[16:]], 0)
        beside.append(jnp.concatenate([
            jnp.concatenate([one[:half], middle], 0),
            jnp.concatenate([sines, one[half + 16 :], nothing], 0),
        ], 1))
    whole = dot(jnp.concatenate(beside, 0), forward)
    return [whole[k * rows : (k + 1) * rows] for k in range(len(halves))]


def flows_of(sides, signs, mixer, back):
    rows, side = sides[0][0].shape[0], back.shape[0]
    half = side // 2
    powers = []
    for (moving, fixed), sign in zip(sides, signs):
        mr, mi, fr, fi = moving[:, :side], moving[:, side:], fixed[:, :side], fixed[:, side:]
        imag = mi * fr - mr * fi
        powers.append(
            jnp.concatenate([mr * fr + mi * fi, imag if sign is None else imag * sign], 1).astype(BF16)
        )
    mixed = dot(jnp.concatenate(powers, 0), mixer)
    top = lax.broadcasted_iota(jnp.int32, (8, side), 0) == 0
    stacks = []
    for k in range(len(sides)):
        one = mixed[k * rows : (k + 1) * rows]
        first, second = one[:, :side], one[:, side:]
        swap = jnp.where(top, first[half : half + 8], second[:8])
        stacks.append(jnp.concatenate([first[:half], swap, second[8:half]], 0).astype(BF16))
    lag = lag_of((side, side), 0, side)
    plain, by_row = [], []
    for k in range(0, len(sides), 2):
        surface = dot(back, jnp.concatenate([stacks[k], stacks[k + 1]], 1))
        for at in (slice(0, side), slice(side, 2 * side)):
            weight = surface[:, at] * surface[:, at]
            plain.append(jnp.sum(weight, 0, keepdims=True))
            by_row.append(jnp.sum(lag * weight, 0, keepdims=True))
    plain = jnp.concatenate(plain, 0)
    by_row = jnp.concatenate(by_row, 0)
    scale = 1.0 / (side * side)
    denom = jnp.sum(plain, 1, keepdims=True) * scale + 1e-06
    flow_y = jnp.sum(by_row, 1, keepdims=True) * scale / denom
    flow_x = jnp.sum(plain * lag_of(plain.shape, 1, side), 1, keepdims=True) * scale / denom
    return flow_y, flow_x


def first_kernel(
    order, cap, slots_ref, links_ref, x, table, spec, mix_ref, place_ref, meta_ref, base_ref
):
    count = len(order)
    total = count * cap
    pairs = slots_ref.shape[-1]
    shift = cap.bit_length() - 1
    me = lax.axis_index("tiles")

    for source in range(count):
        off = offset_from(source, me, count)
        at = jnp.int32(0)
        for k, d in enumerate(order):
            at = jnp.where(off == d, k * cap, at)
        base_ref[source] = at
    base_ref[count] = total
    for s in range(2 * cap + 1):
        meta_ref[0, s] = -1
        meta_ref[1, s] = 0
        meta_ref[2, s] = total
    late = (count - 2) * cap
    for q in range(pairs):
        a, b = slots_ref[0, 0, q], slots_ref[0, 1, q]
        a = base_ref[a >> shift] + (a & (cap - 1))
        b = base_ref[b >> shift] + (b & (cap - 1))
        place_ref[0, q] = a
        place_ref[1, q] = b
        at = jnp.where((a >= late) & (a < total), a - late, 2 * cap)
        meta_ref[0, at] = q
        meta_ref[1, at] = 1
        meta_ref[2, at] = b
        at = jnp.where((b >= late) & (b < total), b - late, 2 * cap)
        meta_ref[0, at] = q
        meta_ref[1, at] = -1
        meta_ref[2, at] = a

    row = lax.broadcasted_iota(jnp.int32, mix_ref.shape, 0)
    links = links_ref.shape[1]
    mix = jnp.zeros(mix_ref.shape, F32)
    for k in range(links):
        share = 0.5 if k == 0 else 0.5 / (links - 1)
        mix += jnp.where(row == links_ref[0, k : k + 1, :], share, 0.0)
    mix_ref[...] = mix

    spec[late:] = jnp.zeros((spec.shape[0] - late,) + spec.shape[1:], F32)
    fill(spec, 0, x, table)


def fill(spec, start, x, table):
    cap = x.shape[0]
    tables = split_table(table)
    halves = halves_of([x[s] for s in range(cap)], *tables[:3])
    for s, one in enumerate(spectra(halves, tables[3])):
        spec[start * cap + s] = one


def next_kernel(start, *refs):
    table, chunks, spec = refs[1], refs[2:-1], refs[-1]
    for k, x in enumerate(chunks):
        fill(spec, start + k, x, table)


def early_kernel(start, spec_in, table, place_ref, x, spec, flow_ref):
    pairs = place_ref.shape[-1]
    side = x.shape[-1]
    fill(spec, start, x, table)

    @pl.loop(0, pairs // GROUP)
    def _(g):
        sides = [
            (spec[place_ref[0, g * GROUP + j]], spec[place_ref[1, g * GROUP + j]])
            for j in range(GROUP)
        ]
        mixer, back = split_table(table)[4:]
        flow_y, flow_x = flows_of(sides, [None] * GROUP, mixer, back)
        for j in range(GROUP):
            at = pl.ds(g * GROUP + j, 1)
            flow_ref[0, at] = jnp.broadcast_to(flow_y[j : j + 1], (1, side))
            flow_ref[1, at] = jnp.broadcast_to(flow_x[j : j + 1], (1, side))


def late_flows(halves, others, base, flow_in, meta_ref, table):
    cap, side = halves.shape[0], halves.shape[-1]
    pairs = flow_in.shape[1]
    forward, mixer, back = split_table(table)[3:]
    own = spectra([halves[s] for s in range(cap)], forward)
    signs = [meta_ref[1, base + s].astype(F32) for s in range(cap)]
    late = flows_of([(own[s], others[s]) for s in range(cap)], signs, mixer, back)
    row = lax.broadcasted_iota(jnp.int32, (pairs, side), 0)
    outs = []
    for c in range(2):
        out = flow_in[c]
        for s in range(cap):
            out = jnp.where(row == meta_ref[0, base + s], late[c][s : s + 1], out)
        outs.append(out)
    return own, outs


def late_kernel(start, spec_in, table, meta_ref, halves, flow_in, spec, flow_ref, other_ref):
    cap = halves.shape[0]
    others = [spec[meta_ref[2, s]] for s in range(cap)]
    own, outs = late_flows(halves, others, 0, flow_in, meta_ref, table)
    for s in range(cap):
        spec[start * cap + s] = own[s]
    for c in range(2):
        flow_ref[c] = outs[c]
    for s in range(cap):
        other_ref[s] = spec[meta_ref[2, cap + s]]


def last_kernel(halves, flow_in, other, meta_ref, table, flow_ref, pair_ref):
    cap, side = halves.shape[0], halves.shape[-1]
    pairs = flow_in.shape[1]
    own, outs = late_flows(halves, [other[s] for s in range(cap)], cap, flow_in, meta_ref, table)
    row = lax.broadcasted_iota(jnp.int32, (pairs, side), 0)
    diagonal = row == lax.broadcasted_iota(jnp.int32, (pairs, side), 1)
    for c in range(2):
        flow_ref[c] = outs[c]
        line = jnp.sum(jnp.where(diagonal, outs[c], 0.0), 0, keepdims=True)
        pair_ref[c : c + 1] = line[:, :pairs]


def relax_kernel(flow_ref, mix_ref, out_ref):
    mix = mix_ref[...]
    for c in range(2):
        flow = jnp.concatenate([flow_ref[m, c] for m in range(flow_ref.shape[0])], 0)
        out_ref[c : c + 1] = jnp.sum(flow * mix, 0, keepdims=True)


def near(x):
    return pltpu.with_memory_space_constraint(x, pltpu.VMEM)


def far(x):
    return pltpu.with_memory_space_constraint(x, pltpu.HBM)


def near_scalars(x):
    return pltpu.with_memory_space_constraint(x, pltpu.SMEM)


def route(d, count):
    return [(i, target(i, d, count)) for i in range(count)]


def direct(patches, send_index, pair_slots, node_links):
    side = patches.shape[-1]
    pairs = pair_slots.shape[-1]
    nodes = node_links.shape[-1]
    count = lax.axis_size("tiles")
    meshes = lax.axis_size("mesh")
    cap = send_index.shape[-1] // count
    order = [0] + offsets(count)
    total = count * cap
    rows = half_rows(side)
    table = half_tables(side)
    send_index, patches, table = far(send_index), far(patches), far(table)
    chunk = pltpu.VMEM((cap, side, side), patches.dtype)
    lead = pl.pallas_call(
        functools.partial(pick_first_kernel, order, cap),
        out_shape=chunk,
        in_specs=[SMEM, ANY],
        out_specs=VMEM,
        scratch_shapes=[pltpu.SemaphoreType.DMA((cap,))],
        compiler_params=PARAMS,
        name="pick_first",
    )(send_index, patches)
    sent = [None] * count
    sent[1] = lax.ppermute(lead, "tiles", route(order[1], count))
    *picked, table = pl.pallas_call(
        functools.partial(pick_rest_kernel, order, cap),
        out_shape=[chunk] * (count - 1) + [pltpu.VMEM(table.shape, table.dtype)],
        in_specs=[SMEM, ANY, ANY],
        out_specs=[VMEM] * count,
        scratch_shapes=[
            pltpu.VMEM((2, cap, side, side), patches.dtype),
            pltpu.SemaphoreType.DMA(((count - 1) * cap,)),
            pltpu.SemaphoreType.DMA,
        ],
        compiler_params=PARAMS,
        name="pick_rest",
    )(send_index, patches, table)
    for k in range(2, count):
        sent[k] = lax.ppermute(picked[k - 1], "tiles", route(order[k], count))
    sent[0] = picked[0]
    chunks = [near(c) for c in sent]
    table = near(table)

    spec_shape = pltpu.VMEM((total + 1, rows, 2 * side), F32)
    flow_shape = pltpu.VMEM((2, pairs, side), F32)
    spec, mix, place, meta = pl.pallas_call(
        functools.partial(first_kernel, order, cap),
        out_shape=[
            spec_shape,
            pltpu.VMEM((meshes * pairs, nodes), F32),
            pltpu.SMEM((2, pairs), jnp.int32),
            pltpu.SMEM((3, 2 * cap + 1), jnp.int32),
        ],
        in_specs=[SMEM, VMEM, VMEM, VMEM],
        out_specs=[VMEM, VMEM, SMEM, SMEM],
        scratch_shapes=[pltpu.SMEM((count + 1,), jnp.int32)],
        compiler_params=PARAMS,
        name="first",
    )(far(pair_slots), far(node_links), chunks[0], table)
    place, meta = near_scalars(place), near_scalars(meta)
    for start, stop in STAGES if count == 8 else ((1, count - 3),):
        if start >= stop:
            continue
        spec = pl.pallas_call(
            functools.partial(next_kernel, start),
            out_shape=spec_shape,
            in_specs=[VMEM] * (2 + stop - start),
            out_specs=VMEM,
            input_output_aliases={0: 0},
            compiler_params=PARAMS,
            name=f"next{start}",
        )(near(spec), table, *chunks[start:stop])
    spec, flow = pl.pallas_call(
        functools.partial(early_kernel, count - 3),
        out_shape=[spec_shape, flow_shape],
        in_specs=[VMEM, VMEM, SMEM, VMEM],
        out_specs=[VMEM, VMEM],
        input_output_aliases={0: 0},
        compiler_params=PARAMS,
        name="early",
    )(near(spec), table, place, chunks[-3])
    spec, flow, other = pl.pallas_call(
        functools.partial(late_kernel, count - 2),
        out_shape=[spec_shape, flow_shape, pltpu.VMEM((cap, rows, 2 * side), F32)],
        in_specs=[VMEM, VMEM, SMEM, VMEM, VMEM],
        out_specs=[VMEM, VMEM, VMEM],
        input_output_aliases={0: 0},
        compiler_params=PARAMS,
        name="late",
    )(near(spec), table, meta, chunks[-2], near(flow))
    flow, pair_flow = pl.pallas_call(
        last_kernel,
        out_shape=[flow_shape, jax.ShapeDtypeStruct((2, pairs), F32)],
        in_specs=[VMEM, VMEM, VMEM, SMEM, VMEM],
        out_specs=[VMEM, VMEM],
        compiler_params=PARAMS,
        name="last",
    )(chunks[-1], near(flow), near(other), meta, table)
    both = lax.all_gather(flow, "mesh")
    relaxed = pl.pallas_call(
        relax_kernel,
        out_shape=jax.ShapeDtypeStruct((2, nodes), F32),
        in_specs=[VMEM, VMEM],
        out_specs=VMEM,
        compiler_params=PARAMS,
        name="relax",
    )(near(both), near(mix))
    return pair_flow, relaxed


def general(patches, send_index, pair_slots, node_links):
    side = patches.shape[-1]
    held = patches.shape[0]
    pairs = pair_slots.shape[-1]
    count = lax.axis_size("tiles")
    band, left, right, back = make_tables(side)
    wanted = send_index[0]
    cap = wanted.shape[0] // count
    picked = patches[jnp.minimum(wanted, held - 1)]
    picked = jnp.where((wanted < held)[:, None, None], picked, jnp.zeros_like(picked))
    received = lax.all_to_all(
        picked.reshape((count, cap) + patches.shape[1:]), "tiles", 0, 0, tiled=True
    )
    total = count * cap
    received = received.reshape((total,) + received.shape[2:])
    slots = pair_slots[0].reshape(-1)
    chosen = received[jnp.minimum(slots, total - 1)]
    chosen = jnp.where((slots < total)[:, None, None], chosen, jnp.zeros_like(chosen))

    def mul(form, a, b):
        return jnp.einsum(form, a, b, preferred_element_type=F32)

    partial = mul("ij,bjk->bik", band, chosen).astype(BF16)
    filtered = mul("bij,kj->bik", partial, band).astype(BF16)
    halves = mul("ij,bjk->bik", left, filtered).astype(BF16)
    quarter = mul("bij,jk->bik", halves, right)
    real = quarter[:, :side, :side] - quarter[:, side:, side:]
    imag = -(quarter[:, :side, side:] + quarter[:, side:, :side])
    mr, fr, mi, fi = real[:pairs], real[pairs:], imag[:pairs], imag[pairs:]
    power = jnp.concatenate([mr * fr + mi * fi, mi * fr - mr * fi], 1).astype(BF16)
    mixed = mul("bij,jk->bik", power, right)
    first = mixed[:, :side, :side] - mixed[:, side:, side:]
    second = mixed[:, :side, side:] + mixed[:, side:, :side]
    stacked = jnp.concatenate([first, second], 1).astype(BF16)
    weight = mul("ij,bjk->bik", back, stacked) ** 2
    lag = jnp.asarray(np.where(np.arange(side) < side / 2, 0, -side) + np.arange(side), F32)
    denom = jnp.mean(weight, axis=(1, 2)) + 1e-06
    flow_y = jnp.mean(lag[None, :, None] * weight, axis=(1, 2)) / denom
    flow_x = jnp.mean(lag[None, None, :] * weight, axis=(1, 2)) / denom
    pair_flow = jnp.stack([flow_y, flow_x], 0)
    rows = lax.all_gather(pair_flow, "mesh", axis=1, tiled=True)
    linked = rows[:, node_links[0]]
    relaxed = 0.5 * linked[:, 0] + 0.5 * jnp.mean(linked[:, 1:], axis=1)
    return pair_flow, relaxed

def per_device(patches, send_index, pair_slots, node_links):
    count = lax.axis_size("tiles")
    cap = send_index.shape[-1] // count
    pairs = pair_slots.shape[-1]
    few = 2 < count <= DIRECT_LIMIT and count & (count - 1) == 0
    if few and cap % 2 == 0 and cap & (cap - 1) == 0 and pairs % GROUP == 0:
        return direct(patches, send_index, pair_slots, node_links)
    return general(patches, send_index, pair_slots, node_links)


def solution(mesh):
    split = ("parts", "tiles", "mesh")
    return jax.shard_map(
        per_device,
        mesh=mesh,
        in_specs=(P(split, None, None), P(split, None), P(split, None, None), P(split, None, None)),
        out_specs=(P(None, split), P(None, split)),
        check_vma=False,
    )
```

```python
import functools
import math

import jax
import jax.numpy as jnp
import numpy as np
from jax import lax
from jax.experimental import pallas as pl
from jax.experimental.pallas import tpu as pltpu
from jax.sharding import PartitionSpec as P


F32 = jnp.float32
BF16 = jnp.bfloat16
ANY = pl.BlockSpec(memory_space=pl.ANY)
SMEM = pl.BlockSpec(memory_space=pltpu.SMEM)
VMEM = pl.BlockSpec(memory_space=pltpu.VMEM)
DIRECT_LIMIT = 16


def const(array):
    return jnp.asarray(array.astype(np.float32)).astype(BF16)


def base_tables(side):
    ticks = np.arange(side)
    angle = 2.0 * np.pi / side * (ticks[:, None] * ticks[None, :] % side)
    cosine = np.cos(angle) / math.sqrt(side)
    sine = np.sin(angle) / math.sqrt(side)
    gap = (ticks[:, None] - ticks[None, :]).astype(np.float64)
    narrow = np.exp(-gap * gap / (2.0 * 0.35 * 0.35)) / (0.35 * math.sqrt(2.0 * math.pi))
    broad = np.exp(-gap * gap / 32.0) / (4.0 * math.sqrt(2.0 * math.pi))
    return cosine, sine, narrow - broad


def make_tables(side):
    cosine, sine, band = base_tables(side)
    left = np.concatenate([cosine, sine], 0)
    right = np.concatenate([cosine, sine], 1)
    back = np.concatenate([cosine, -sine], 1)
    return const(band), const(left), const(right), const(back)


def half_rows(side):
    return -(-(side // 2 + 1) // 16) * 16


def half_tables(side):
    cosine, sine, band = base_tables(side)
    half = side // 2
    zero = np.zeros((side, side))
    band_pair = np.block([[band.T, zero], [zero, band.T]])
    left = np.concatenate([cosine[: half + 1], sine[1:half]], 0)
    forward = np.block([[cosine, -sine], [-sine, -cosine]])
    mixer = np.block([[cosine, sine], [-sine, cosine]])
    back = np.concatenate([2.0 * cosine[:, :half], -2.0 * sine[:, :half]], 1)
    back[:, 0] = cosine[:, 0]
    back[:, half] = cosine[:, half]
    small = np.concatenate([band, back], 1)
    left = np.concatenate([left, zero], 1)
    return const(np.concatenate([band_pair, forward, mixer, small, left], 0))


def split_table(table):
    side = table.shape[-1] // 2
    forward, mixer, small, left = 2 * side, 4 * side, 6 * side, 7 * side
    return (
        table[small:left, :side],
        table[:forward, :],
        table[left:, :side],
        table[forward:mixer, :],
        table[mixer:small, :],
        table[small:left, side:],
    )


def dot(a, b):
    return jnp.dot(a, b, preferred_element_type=F32)


def lag_of(shape, dim, side):
    place = lax.broadcasted_iota(jnp.int32, shape, dim).astype(F32)
    return jnp.where(place < side / 2, place, place - side)


GROUP = 4
LEAD = 2
LATE = 5
PARAMS = pltpu.CompilerParams(vmem_limit_bytes=8 * 2**20)


MODE = "xor"


def offsets(count):
    if count == 8:
        return [4, 5, 2, 3, 1, 6, 7]
    return list(range(count - 1, 0, -1))


def turns(count):
    if count == 8:
        return [0, 4, 1, 5, 2, 3, 6, 7]
    return [0] + offsets(count)


def gray(place):
    return place ^ (place >> 1)


def target(me, d, count):
    if MODE == "xor":
        return me ^ d
    if MODE == "gray":
        at = (gray(me >> 1) + (d >> 1)) & (count // 2 - 1)
        return (gray(at) << 1) + ((me ^ d) & 1)
    if MODE == "shift":
        return (me + d) & (count - 1)
    return ((((me >> 1) + (d >> 1)) & (count // 2 - 1)) << 1) + ((me ^ d) & 1)


def offset_from(source, me, count):
    if MODE == "xor":
        return me ^ source
    if MODE == "gray":
        at = (gray(me >> 1) - gray(source >> 1)) & (count // 2 - 1)
        return (at << 1) + ((me ^ source) & 1)
    if MODE == "shift":
        return (me - source) & (count - 1)
    return ((((me >> 1) - (source >> 1)) & (count // 2 - 1)) << 1) + ((me ^ source) & 1)


def chosen(held, send_ref, d, count, cap):
    peer = target(lax.axis_index("tiles"), d, count)
    limit = held.shape[0]
    result = []
    for s in range(cap):
        index = send_ref[0, peer * cap + s]
        keep = jnp.where(index < limit, 1.0, 0.0).astype(BF16)
        result.append(held[jnp.minimum(index, limit - 1)] * keep)
    return result


def pick_first_kernel(offs, count, cap, send_ref, patches_ref, *rest):
    outs, index_ref, sems = rest[:-2], rest[-2], rest[-1]
    me = lax.axis_index("tiles")
    limit = patches_ref.shape[0]
    copies, indices = [], []
    for d, out in zip(offs, outs):
        peer = target(me, d, count)
        for s in range(cap):
            index = send_ref[0, peer * cap + s]
            source = patches_ref.at[jnp.minimum(index, limit - 1)]
            copies.append(pltpu.make_async_copy(source, out.at[s], sems.at[len(copies)]))
            copies[-1].start()
            indices.append(index)
    for k in range(send_ref.shape[1]):
        index_ref[0, k] = send_ref[0, k]
    most = functools.reduce(jnp.maximum, indices)
    for copy in copies:
        copy.wait()

    @pl.when(most >= limit)
    def _():
        for n, index in enumerate(indices):
            keep = jnp.where(index < limit, 1.0, 0.0).astype(BF16)
            out = outs[n // cap]
            out[n % cap] = out[n % cap] * keep


def pick_rest_kernel(offs, late, count, cap, send_ref, patches_ref, far_table, *rest):
    outs, table = rest[: len(offs)], rest[len(offs)]
    held, sems, sem = rest[len(offs) + 1 :]
    lots = sems.shape[0]
    step = held.shape[0] // lots
    copies = []
    for k in range(lots):
        at = pl.ds(k * step, step)
        copies.append(pltpu.make_async_copy(patches_ref.at[at], held.at[at], sems.at[k]))
        copies[-1].start()
    copy = pltpu.make_async_copy(far_table, table, sem)
    copy.start()
    for one in copies:
        one.wait()
    for d, out in zip(offs, outs):
        if d not in late:
            for s, one in enumerate(chosen(held, send_ref, d, count, cap)):
                out[s] = one
    copy.wait()
    for d, out in zip(offs, outs):
        if d in late:
            halves = halves_of(chosen(held, send_ref, d, count, cap), *split_table(table)[:3])
            for s in range(cap):
                out[s] = halves[s]


def halves_of(x, band, band_pair, left):
    side = x[0].shape[-1]
    result = []
    for k in range(0, len(x), 2):
        both = jnp.concatenate([x[k], x[k + 1]], 1)
        partial = dot(band, both).astype(BF16)
        filtered = dot(partial, band_pair).astype(BF16)
        halves = dot(left, filtered).astype(BF16)
        result += [halves[:, :side], halves[:, side:]]
    return result


def spectra(halves, forward):
    side = halves[0].shape[-1]
    half, rows = side // 2, half_rows(side)
    top = lax.broadcasted_iota(jnp.int32, (16, side), 0) == 0
    nothing = jnp.zeros((rows - half, side), BF16)
    beside = []
    for one in halves:
        mixed = one[half : half + 16].astype(F32)
        middle = jnp.where(top, mixed, 0.0).astype(BF16)
        sines = jnp.where(top, 0.0, mixed).astype(BF16)
        if rows - half > 16:
            middle = jnp.concatenate([middle, nothing[16:]], 0)
        beside.append(jnp.concatenate([
            jnp.concatenate([one[:half], middle], 0),
            jnp.concatenate([sines, one[half + 16 :], nothing], 0),
        ], 1))
    whole = dot(jnp.concatenate(beside, 0), forward)
    return [whole[k * rows : (k + 1) * rows] for k in range(len(halves))]


def flows_of(sides, signs, mixer, back):
    rows, side = sides[0][0].shape[0], back.shape[0]
    half = side // 2
    powers = []
    for (moving, fixed), sign in zip(sides, signs):
        mr, mi, fr, fi = moving[:, :side], moving[:, side:], fixed[:, :side], fixed[:, side:]
        imag = mi * fr - mr * fi
        powers.append(
            jnp.concatenate([mr * fr + mi * fi, imag if sign is None else imag * sign], 1).astype(BF16)
        )
    mixed = dot(jnp.concatenate(powers, 0), mixer)
    top = lax.broadcasted_iota(jnp.int32, (8, side), 0) == 0
    stacks = []
    for k in range(len(sides)):
        one = mixed[k * rows : (k + 1) * rows]
        first, second = one[:, :side], one[:, side:]
        swap = jnp.where(top, first[half : half + 8], second[:8])
        stacks.append(jnp.concatenate([first[:half], swap, second[8:half]], 0).astype(BF16))
    lag = lag_of((side, side), 0, side)
    plain, by_row = [], []
    for k in range(0, len(sides), 2):
        surface = dot(back, jnp.concatenate([stacks[k], stacks[k + 1]], 1))
        for at in (slice(0, side), slice(side, 2 * side)):
            weight = surface[:, at] * surface[:, at]
            plain.append(jnp.sum(weight, 0, keepdims=True))
            by_row.append(jnp.sum(lag * weight, 0, keepdims=True))
    plain = jnp.concatenate(plain, 0)
    by_row = jnp.concatenate(by_row, 0)
    scale = 1.0 / (side * side)
    denom = jnp.sum(plain, 1, keepdims=True) * scale + 1e-06
    flow_y = jnp.sum(by_row, 1, keepdims=True) * scale / denom
    flow_x = jnp.sum(plain * lag_of(plain.shape, 1, side), 1, keepdims=True) * scale / denom
    return flow_y, flow_x


def first_kernel(
    order, cap, slots_ref, links_ref, x, table, spec, mix_ref, place_ref, meta_ref, base_ref
):
    count = len(order)
    total = count * cap
    pairs = slots_ref.shape[-1]
    shift = cap.bit_length() - 1
    me = lax.axis_index("tiles")

    for source in range(count):
        off = offset_from(source, me, count)
        at = jnp.int32(0)
        for k, d in enumerate(order):
            at = jnp.where(off == d, k * cap, at)
        base_ref[source] = at
    base_ref[count] = total
    for s in range(LATE * cap + 1):
        meta_ref[0, s] = -1
        meta_ref[1, s] = 0
        meta_ref[2, s] = total
    late = (count - LATE) * cap
    for q in range(pairs):
        a, b = slots_ref[0, 0, q], slots_ref[0, 1, q]
        a = base_ref[a >> shift] + (a & (cap - 1))
        b = base_ref[b >> shift] + (b & (cap - 1))
        place_ref[0, q] = a
        place_ref[1, q] = b
        at = jnp.where((a >= late) & (a < total), a - late, LATE * cap)
        meta_ref[0, at] = q
        meta_ref[1, at] = 1
        meta_ref[2, at] = b
        at = jnp.where((b >= late) & (b < total), b - late, LATE * cap)
        meta_ref[0, at] = q
        meta_ref[1, at] = -1
        meta_ref[2, at] = a

    row = lax.broadcasted_iota(jnp.int32, mix_ref.shape, 0)
    links = links_ref.shape[1]
    mix = jnp.zeros(mix_ref.shape, F32)
    for k in range(links):
        share = 0.5 if k == 0 else 0.5 / (links - 1)
        mix += jnp.where(row == links_ref[0, k : k + 1, :], share, 0.0)
    mix_ref[...] = mix

    spec[late:] = jnp.zeros((spec.shape[0] - late,) + spec.shape[1:], F32)
    fill(spec, 0, x, table)


def fill(spec, start, x, table):
    cap = x.shape[0]
    tables = split_table(table)
    halves = halves_of([x[s] for s in range(cap)], *tables[:3])
    for s, one in enumerate(spectra(halves, tables[3])):
        spec[start * cap + s] = one


def next_kernel(start, *refs):
    table, chunks, spec = refs[1], refs[2:-1], refs[-1]
    for k, x in enumerate(chunks):
        fill(spec, start + k, x, table)


def early_kernel(start, spec_in, table, place_ref, x, spec, flow_ref):
    pairs = place_ref.shape[-1]
    side = x.shape[-1]
    fill(spec, start, x, table)

    @pl.loop(0, pairs // GROUP)
    def _(g):
        sides = [
            (spec[place_ref[0, g * GROUP + j]], spec[place_ref[1, g * GROUP + j]])
            for j in range(GROUP)
        ]
        mixer, back = split_table(table)[4:]
        flow_y, flow_x = flows_of(sides, [None] * GROUP, mixer, back)
        for j in range(GROUP):
            at = pl.ds(g * GROUP + j, 1)
            flow_ref[0, at] = jnp.broadcast_to(flow_y[j : j + 1], (1, side))
            flow_ref[1, at] = jnp.broadcast_to(flow_x[j : j + 1], (1, side))


def late_flows(turn, spec, table, meta_ref, halves, flow_in):
    cap, side = halves.shape[0], halves.shape[-1]
    pairs = flow_in.shape[1]
    forward, mixer, back = split_table(table)[3:]
    base = turn * cap
    own = spectra([halves[s] for s in range(cap)], forward)
    sides = [(own[s], spec[meta_ref[2, base + s]]) for s in range(cap)]
    signs = [meta_ref[1, base + s].astype(F32) for s in range(cap)]
    late = flows_of(sides, signs, mixer, back)
    row = lax.broadcasted_iota(jnp.int32, (pairs, side), 0)
    outs = []
    for c in range(2):
        out = flow_in[c]
        for s in range(cap):
            out = jnp.where(row == meta_ref[0, base + s], late[c][s : s + 1], out)
        outs.append(out)
    return own, outs


def late_kernel(turn, start, spec_in, table, meta_ref, halves, flow_in, spec, flow_ref):
    own, outs = late_flows(turn, spec, table, meta_ref, halves, flow_in)
    cap = halves.shape[0]
    for s in range(cap):
        spec[start * cap + s] = own[s]
    for c in range(2):
        flow_ref[c] = outs[c]


def last_kernel(turn, spec, table, meta_ref, halves, flow_in, flow_ref):
    _, outs = late_flows(turn, spec, table, meta_ref, halves, flow_in)
    for c in range(2):
        flow_ref[c] = outs[c]


def relax_kernel(own_ref, other_ref, mix_ref, out_ref, pair_ref):
    pairs, side = own_ref.shape[1:]
    me = lax.axis_index("mesh")
    own_mix = mix_ref[pl.ds(me * pairs, pairs)]
    other_mix = mix_ref[pl.ds((1 - me) * pairs, pairs)]
    row = lax.broadcasted_iota(jnp.int32, (pairs, side), 0)
    diagonal = row == lax.broadcasted_iota(jnp.int32, (pairs, side), 1)
    for c in range(2):
        own = own_ref[c]
        line = jnp.sum(jnp.where(diagonal, own, 0.0), 0, keepdims=True)
        pair_ref[c : c + 1] = line[:, :pairs]
        mixed = own * own_mix + other_ref[c] * other_mix
        out_ref[c : c + 1] = jnp.sum(mixed, 0, keepdims=True)


def near(x):
    return pltpu.with_memory_space_constraint(x, pltpu.VMEM)


def far(x):
    return pltpu.with_memory_space_constraint(x, pltpu.HBM)


def near_scalars(x):
    return pltpu.with_memory_space_constraint(x, pltpu.SMEM)


def send(x, d, count):
    return lax.ppermute(x, "tiles", [(i, target(i, d, count)) for i in range(count)])


def direct(patches, send_index, pair_slots, node_links):
    side = patches.shape[-1]
    pairs = pair_slots.shape[-1]
    nodes = node_links.shape[-1]
    count = lax.axis_size("tiles")
    meshes = lax.axis_size("mesh")
    cap = send_index.shape[-1] // count
    issue, order = offsets(count), turns(count)
    late = order[-LATE:]
    total = count * cap
    rows = half_rows(side)
    table = half_tables(side)
    send_index, patches, table = far(send_index), far(patches), far(table)
    chunk = pltpu.VMEM((cap, side, side), patches.dtype)
    lead = [d for k, d in enumerate(issue) if k < LEAD and d not in late]
    lots = math.gcd(patches.shape[0], 4)
    *picked, index = pl.pallas_call(
        functools.partial(pick_first_kernel, lead, count, cap),
        out_shape=[chunk] * len(lead) + [pltpu.SMEM(send_index.shape, send_index.dtype)],
        in_specs=[SMEM, ANY],
        out_specs=[VMEM] * len(lead) + [SMEM],
        scratch_shapes=[pltpu.SemaphoreType.DMA((len(lead) * cap,))],
        compiler_params=PARAMS,
        name="pick_first",
    )(send_index, patches)
    sent = {d: send(one, d, count) for d, one in zip(lead, picked)}
    offs = [d for d in [0] + issue if d not in lead]
    *picked, table = pl.pallas_call(
        functools.partial(pick_rest_kernel, offs, late, count, cap),
        out_shape=[chunk] * len(offs) + [pltpu.VMEM(table.shape, table.dtype)],
        in_specs=[SMEM, ANY, ANY],
        out_specs=[VMEM] * (len(offs) + 1),
        scratch_shapes=[
            pltpu.VMEM(patches.shape, patches.dtype),
            pltpu.SemaphoreType.DMA((lots,)),
            pltpu.SemaphoreType.DMA,
        ],
        compiler_params=PARAMS,
        name="pick_rest",
    )(near_scalars(index), patches, table)
    for d, one in zip(offs, picked):
        sent[d] = send(one, d, count) if d else one
    chunks = [near(sent[d]) for d in order]
    table = near(table)

    spec_shape = pltpu.VMEM((total + 1, rows, 2 * side), F32)
    flow_shape = pltpu.VMEM((2, pairs, side), F32)
    spec, mix, place, meta = pl.pallas_call(
        functools.partial(first_kernel, order, cap),
        out_shape=[
            spec_shape,
            pltpu.VMEM((meshes * pairs, nodes), F32),
            pltpu.SMEM((2, pairs), jnp.int32),
            pltpu.SMEM((3, LATE * cap + 1), jnp.int32),
        ],
        in_specs=[SMEM, VMEM, VMEM, VMEM],
        out_specs=[VMEM, VMEM, SMEM, SMEM],
        scratch_shapes=[pltpu.SMEM((count + 1,), jnp.int32)],
        compiler_params=PARAMS,
        name="first",
    )(far(pair_slots), far(node_links), chunks[0], table)
    place, meta = near_scalars(place), near_scalars(meta)
    for k in range(1, count - LATE - 1):
        spec = pl.pallas_call(
            functools.partial(next_kernel, k),
            out_shape=spec_shape,
            in_specs=[VMEM] * 3,
            out_specs=VMEM,
            input_output_aliases={0: 0},
            compiler_params=PARAMS,
        )(near(spec), table, chunks[k])
    spec, flow = pl.pallas_call(
        functools.partial(early_kernel, count - LATE - 1),
        out_shape=[spec_shape, flow_shape],
        in_specs=[VMEM, VMEM, SMEM, VMEM],
        out_specs=[VMEM, VMEM],
        input_output_aliases={0: 0},
        compiler_params=PARAMS,
        name="early",
    )(near(spec), table, place, chunks[count - LATE - 1])
    for turn in range(LATE - 1):
        k = count - LATE + turn
        spec, flow = pl.pallas_call(
            functools.partial(late_kernel, turn, k),
            out_shape=[spec_shape, flow_shape],
            in_specs=[VMEM, VMEM, SMEM, VMEM, VMEM],
            out_specs=[VMEM, VMEM],
            input_output_aliases={0: 0},
            compiler_params=PARAMS,
        )(near(spec), table, meta, chunks[k], near(flow))
    flow = pl.pallas_call(
        functools.partial(last_kernel, LATE - 1),
        out_shape=flow_shape,
        in_specs=[VMEM, VMEM, SMEM, VMEM, VMEM],
        out_specs=VMEM,
        compiler_params=PARAMS,
        name="last",
    )(near(spec), table, meta, chunks[-1], near(flow))
    other = lax.ppermute(flow, "mesh", [(0, 1), (1, 0)])
    relaxed, pair_flow = pl.pallas_call(
        relax_kernel,
        out_shape=[
            jax.ShapeDtypeStruct((2, nodes), F32),
            jax.ShapeDtypeStruct((2, pairs), F32),
        ],
        in_specs=[VMEM, VMEM, VMEM],
        out_specs=[VMEM, VMEM],
        compiler_params=PARAMS,
        name="relax",
    )(near(flow), near(other), near(mix))
    return pair_flow, relaxed


def general(patches, send_index, pair_slots, node_links):
    side = patches.shape[-1]
    held = patches.shape[0]
    pairs = pair_slots.shape[-1]
    count = lax.axis_size("tiles")
    band, left, right, back = make_tables(side)
    wanted = send_index[0]
    cap = wanted.shape[0] // count
    picked = patches[jnp.minimum(wanted, held - 1)]
    picked = jnp.where((wanted < held)[:, None, None], picked, jnp.zeros_like(picked))
    received = lax.all_to_all(
        picked.reshape((count, cap) + patches.shape[1:]), "tiles", 0, 0, tiled=True
    )
    total = count * cap
    received = received.reshape((total,) + received.shape[2:])
    slots = pair_slots[0].reshape(-1)
    chosen = received[jnp.minimum(slots, total - 1)]
    chosen = jnp.where((slots < total)[:, None, None], chosen, jnp.zeros_like(chosen))

    def mul(form, a, b):
        return jnp.einsum(form, a, b, preferred_element_type=F32)

    partial = mul("ij,bjk->bik", band, chosen).astype(BF16)
    filtered = mul("bij,kj->bik", partial, band).astype(BF16)
    halves = mul("ij,bjk->bik", left, filtered).astype(BF16)
    quarter = mul("bij,jk->bik", halves, right)
    real = quarter[:, :side, :side] - quarter[:, side:, side:]
    imag = -(quarter[:, :side, side:] + quarter[:, side:, :side])
    mr, fr, mi, fi = real[:pairs], real[pairs:], imag[:pairs], imag[pairs:]
    power = jnp.concatenate([mr * fr + mi * fi, mi * fr - mr * fi], 1).astype(BF16)
    mixed = mul("bij,jk->bik", power, right)
    first = mixed[:, :side, :side] - mixed[:, side:, side:]
    second = mixed[:, :side, side:] + mixed[:, side:, :side]
    stacked = jnp.concatenate([first, second], 1).astype(BF16)
    weight = mul("ij,bjk->bik", back, stacked) ** 2
    lag = jnp.asarray(np.where(np.arange(side) < side / 2, 0, -side) + np.arange(side), F32)
    denom = jnp.mean(weight, axis=(1, 2)) + 1e-06
    flow_y = jnp.mean(lag[None, :, None] * weight, axis=(1, 2)) / denom
    flow_x = jnp.mean(lag[None, None, :] * weight, axis=(1, 2)) / denom
    pair_flow = jnp.stack([flow_y, flow_x], 0)
    rows = lax.all_gather(pair_flow, "mesh", axis=1, tiled=True)
    linked = rows[:, node_links[0]]
    relaxed = 0.5 * linked[:, 0] + 0.5 * jnp.mean(linked[:, 1:], axis=1)
    return pair_flow, relaxed


def is_direct(count, cap, pairs):
    few = LATE + 1 < count <= DIRECT_LIMIT and count & (count - 1) == 0
    return few and cap % 2 == 0 and cap & (cap - 1) == 0 and pairs % GROUP == 0


def per_device(patches, send_index, pair_slots, node_links):
    count = lax.axis_size("tiles")
    fits = is_direct(count, send_index.shape[-1] // count, pair_slots.shape[-1])
    if fits and lax.axis_size("mesh") == 2:
        return direct(patches, send_index, pair_slots, node_links)
    return general(patches, send_index, pair_slots, node_links)


def solution(mesh):
    split = ("parts", "tiles", "mesh")
    return jax.shard_map(
        per_device,
        mesh=mesh,
        in_specs=(P(split, None, None), P(split, None), P(split, None, None), P(split, None, None)),
        out_specs=(P(None, split), P(None, split)),
        check_vma=False,
    )
```
